32 devices in a mesh: grp: 2 (over y), cand: 8 (over z, x), head: 2 (over core).
Axes of the slice: x: 2, y: 2, z: 4, core: 2. Of those that a mesh axis runs over, the one named last changes fastest.
Arguments:
- queries: bfloat16 [8192, 2560], P(('grp', 'cand'), 'head'), parts along dimension 0, may hold values from -130 to 130
- keys: bfloat16 [8192, 512], P(('grp', 'cand'), 'head'), parts along dimension 0, may hold values from -5 to 5
- values: bfloat16 [8192, 512], P(('grp', 'cand'), 'head'), parts along dimension 0, may hold values from -6 to 6
- lengths: int32 [16], P('grp'), parts along dimension 0, may hold values from 257 to 512, as said below
- winners: int32 [8], P('grp'), parts along dimension 0, may hold values from 0 to 1
- score_weight: float32 [2560], P('head'), may hold values from -16 to 16
Outputs:
- first_round: bfloat16 [8192, 2560], P(('grp', 'cand'), 'head'), parts along dimension 0
- second_round: bfloat16 [4096, 2560], P(('grp', 'cand'), 'head'), parts along dimension 0
- first_score: float32 [16], P(('grp', 'cand')), parts along dimension 0
- final_round_score: float32 [16], P(('grp', 'cand')), parts along dimension 0
The draws below stay inside these ranges and needn't reach their ends.
There are 2 independent parts, one for each index of `grp`. The reference program is written for one: setup_inputs(seed, part) draws one part's arguments, and reference() takes and returns one part's arrays. A program takes and returns all parts, laid end to end along the dimension named above; an argument that names none is the same for every part. Nothing has to cross between parts.
Inputs may be any that keep to these rules, and one draw needn't show every extreme that they name: lengths of all candidates lie in this range; some candidate uses all 512 slots. `winners`: 0 picks the even member 2 j of pair j, 1 the odd one.
All inputs are finite; a program needn't handle non-finite values.
Results may differ from the reference program's by a relative error of at most 0.0049.
Values may be sent and summed in bfloat16 or wider, within the bound.
A program may use at most 128 MiB of HBM per device.

```python
import jax
import jax.numpy as jnp
from jax import lax

HQ = 20
KVH = 4
HD = 128
SPAN = 512
CANDS = 8


def shared_keys(key):
    drawn = jax.random.truncated_normal(jax.random.fold_in(key, 11), -5.0, 5.0, (CANDS, SPAN, KVH, HD), jnp.float32)
    return drawn


def draw_keys(key, part):
    return shared_keys(key).reshape(CANDS * SPAN, KVH * HD).astype(jnp.bfloat16)


def draw_queries(key, part):
    base = 1.5 * jax.random.truncated_normal(jax.random.fold_in(key, 12), -5.0, 5.0, (CANDS, SPAN, HQ, HD), jnp.float32)
    return base.reshape(CANDS * SPAN, HQ * HD).astype(jnp.bfloat16)


def draw_lengths(key, part):
    drawn = jax.random.randint(jax.random.fold_in(key, 13), (CANDS,), SPAN // 2 + 1, SPAN + 1, dtype=jnp.int32)
    fullest = jax.random.randint(jax.random.fold_in(key, 14), (), 0, CANDS, dtype=jnp.int32)
    return drawn.at[fullest].set(SPAN)


def draw_score_weight(key, part):
    count = HQ * HD
    ramp = 1.0 + 2.0 * jnp.arange(count, dtype=jnp.float32) / (count - 1)
    drawn = jax.random.truncated_normal(jax.random.fold_in(key, 15), -5.0, 5.0, (count,), jnp.float32) * ramp
    return drawn


def touch_ends(values, stream_key, smallest, high):
    longest = values.shape.index(max(values.shape))
    spots = []
    for shift in (0, 1):
        where = [jax.random.randint(jax.random.fold_in(stream_key, axis), (), 0, length) for axis, length in enumerate(values.shape)]
        where[longest] = (where[longest] + shift) % values.shape[longest]
        spots.append(tuple(where))
    return values.at[spots[0]].set(smallest).at[spots[1]].set(high)


def block_scale(own_key, shape, pieces, low, top_value):
    def one(position, blocks):
        heights = jax.random.uniform(jax.random.fold_in(jax.random.fold_in(own_key, 6), position), (blocks,), jnp.float32, low / len(pieces), top_value / len(pieces))
        return jnp.repeat(jnp.exp(heights), shape[position] // blocks).reshape((-1,) + (1,) * (len(shape) - position - 1))

    factor_of = one(*pieces[0])
    for cut in pieces[1:]:
        factor_of = factor_of * one(*cut)
    return factor_of


def gaussian(own_key, extent, scale, bound, cuts=(), held_as=jnp.bfloat16):
    loudness = block_scale(own_key, extent, cuts, -0.22, 0.18) if cuts else 1.0
    array = jax.random.normal(own_key, extent, jnp.float32) * scale * loudness
    return jnp.minimum(jnp.maximum(array, -bound), bound).astype(held_as)


def setup_inputs(seed: int = 0, part: int = 0) -> dict:
    seeds = jax.random.split(jax.random.key(seed), 7)
    part_splits = jax.random.split(jax.random.fold_in(seeds[6], part), 7)
    return {
        "queries": draw_queries(jax.random.fold_in(jax.random.fold_in(seeds[6], part), 71), part),
        "keys": draw_keys(jax.random.fold_in(jax.random.fold_in(seeds[6], part), 71), part),
        "values": gaussian(part_splits[2], (CANDS * SPAN, KVH * HD), 1.0, 6.0, ((0, 8), (1, 2))),
        "lengths": draw_lengths(jax.random.fold_in(jax.random.fold_in(seeds[6], part), 71), part),
        "winners": touch_ends(jax.random.randint(part_splits[4], (CANDS // 2,), 0, 2), jax.random.fold_in(part_splits[4], 1), 0, 1).astype(jnp.int32),
        "score_weight": draw_score_weight(jax.random.fold_in(seeds[6], 71), part),
    }


def attend_spans(query_rows, key_rows, value_rows, key_valid, valid_row_mask):
    row_count = query_rows.shape[0]
    ratio = HQ // KVH
    grouped_q = query_rows.reshape(row_count, KVH, ratio, HD).transpose(1, 0, 2, 3)
    grouped_k = key_rows.reshape(-1, KVH, HD).transpose(1, 0, 2)
    grouped_v = value_rows.reshape(-1, KVH, HD).transpose(1, 0, 2)

    def one_group(operands):
        queries_g, keys_g, values_g = operands
        scores = jnp.einsum("qrd,kd->rqk", queries_g.astype(jnp.float32), keys_g.astype(jnp.float32)) * (HD ** -0.5)
        scores = jnp.where(key_valid[None, None, :], scores, -jnp.inf)
        peak = jnp.max(scores, axis=2, keepdims=True)
        exps = jnp.exp(scores - peak)
        weights = (exps / jnp.sum(exps, axis=2, keepdims=True)).astype(jnp.bfloat16)
        return jnp.einsum("rqk,kd->qrd", weights.astype(jnp.float32), values_g.astype(jnp.float32))

    outputs = lax.map(one_group, (grouped_q, grouped_k, grouped_v))
    merged = outputs.transpose(1, 0, 2, 3).reshape(row_count, HQ * HD)
    return (merged * valid_row_mask[:, None].astype(jnp.float32)).astype(jnp.bfloat16)


def reference(queries, keys, values, lengths, winners, score_weight):
    cand_q = queries.reshape(CANDS, SPAN, HQ * HD)
    cand_k = keys.reshape(CANDS, SPAN, KVH * HD)
    cand_v = values.reshape(CANDS, SPAN, KVH * HD)
    span_positions = jnp.arange(SPAN, dtype=jnp.int32)
    valid = span_positions[None, :] < lengths[:, None]

    def match_result(pairing_identifiers):
        own = pairing_identifiers[0]
        rival = pairing_identifiers[1]
        key_rows = jnp.concatenate([cand_k[own], cand_k[rival]], axis=0)
        value_rows = jnp.concatenate([cand_v[own], cand_v[rival]], axis=0)
        key_valid = jnp.concatenate([valid[own], valid[rival]], axis=0)
        return attend_spans(cand_q[own], key_rows, value_rows, key_valid, valid[own])

    everyone = jnp.arange(CANDS, dtype=jnp.int32)
    first = lax.map(match_result, jnp.stack([everyone, jnp.bitwise_xor(everyone, 1)], axis=1))
    pairing_identifiers = jnp.arange(CANDS // 2, dtype=jnp.int32)
    remaining_candidates = 2 * pairing_identifiers + winners
    challengers = remaining_candidates[jnp.bitwise_xor(pairing_identifiers, 1)]
    later_round = lax.map(match_result, jnp.stack([remaining_candidates, challengers], axis=1))
    weight = score_weight.astype(jnp.float32)
    first_totals = jnp.sum(first.astype(jnp.float32) * weight, axis=(1, 2))
    first_score = first_totals / lengths.astype(jnp.float32)
    final_round_totals = jnp.sum(later_round.astype(jnp.float32) * weight, axis=(1, 2))
    final_round_score = jnp.repeat(final_round_totals / lengths[remaining_candidates].astype(jnp.float32), 2)
    return (first.reshape(CANDS * SPAN, HQ * HD), later_round.reshape(CANDS // 2 * SPAN, HQ * HD), first_score, final_round_score)
```

```python
import functools

import jax
import jax.numpy as jnp
from jax import lax
from jax.experimental import pallas as pl
from jax.experimental.pallas import tpu as pltpu
from jax.sharding import PartitionSpec as P

HD = 128
LOG2E = 1.4426950408889634
MESH = pl.DeviceIdType.MESH
NEG = -1e30
PAD = 16
OUT = pltpu.VMEM


def kernel(
    heads, groups, span,
    q_hbm, k_hbm, v_hbm, len_hbm, win_hbm, w_hbm,
    o_1, o_2, judged_ref,
    q_v, k_o, v_o, k_x, v_x, q_x, k_s, k_c, v_s, v_c, vt, bias,
    acc, top, len_ref, win_ref, w_ref, part_1, part_2, part_3, got_1, got_2, got_3,
    load_sem, xs, xr, zs, zr, qs, qr, small_sem, ps, pr, z_in, core_in,
):
    half = span // 2
    ratio = heads // groups
    me = lax.axis_index("cand")
    bit = lax.rem(me, 2)
    hd = lax.axis_index("head")
    pair = me // 2
    mate = me + 1 - 2 * bit
    pair_bit = lax.rem(pair, 2)
    rival_pair = pair + 1 - 2 * pair_bit
    across = 2 * rival_pair + bit
    other = 1 - hd

    barrier = pltpu.get_barrier_semaphore()
    pl.semaphore_signal(barrier, inc=1, device_id={"cand": mate}, device_id_type=MESH)
    pl.semaphore_signal(
        barrier, inc=1, device_id={"cand": jnp.where(hd == 0, me, across), "head": 1},
        device_id_type=MESH,
    )

    def col(i):
        return pl.ds(pl.multiple_of(i * HD, HD), HD)

    loads = []
    for g in range(groups):
        loads.append(pltpu.make_async_copy(k_hbm.at[:, col(g)], k_o.at[g], load_sem.at[2 * g]))
        loads.append(pltpu.make_async_copy(v_hbm.at[:, col(g)], v_o.at[g], load_sem.at[2 * g + 1]))
    for h in range(heads):
        loads.append(
            pltpu.make_async_copy(q_hbm.at[:, col(h)], q_v.at[h], load_sem.at[2 * groups + h])
        )
    small = [
        pltpu.make_async_copy(src, dst, small_sem.at[i])
        for i, (src, dst) in enumerate(((len_hbm, len_ref), (win_hbm, win_ref), (w_hbm, w_ref)))
    ]
    pl.semaphore_wait(barrier, 1 + 2 * hd)

    def remote(src, dst, s, r, peer):
        return pltpu.make_async_remote_copy(
            src_ref=src, dst_ref=dst, send_sem=s, recv_sem=r,
            device_id=peer, device_id_type=MESH,
        )

    x_copies, f_copies = [], []
    for g in range(groups):
        for j, (src, dst, fsrc, fdst) in enumerate(
            ((k_hbm, k_x, k_s, k_c), (v_hbm, v_x, v_s, v_c))
        ):
            i = 2 * g + j
            x_copies.append(
                remote(src.at[:, col(g)], dst.at[g], xs.at[i], xr.at[i], {"cand": mate})
            )
            f_copies.append(remote(fsrc.at[g], fdst.at[g], zs.at[i], zr.at[i], {"cand": across}))

    quarter = half // 2
    chunks = [(h, 0, half) for h in range(heads - 1)]
    chunks += [(heads - 1, r, quarter) for r in (0, quarter)]
    q_copies = []
    for i, (h, r, n) in enumerate(chunks):
        rows = pl.ds(pl.multiple_of((1 - bit) * half + r, quarter), n)
        q_copies.append(
            remote(q_hbm.at[rows, col(h)], q_x.at[h, r : r + n], qs.at[i], qr.at[i], {"cand": mate})
        )

    for c in x_copies:
        c.start()
    for c in small + loads:
        c.start()
    for c in q_copies:
        c.start()
    for c in small:
        c.wait()

    @pl.when(hd == 1)
    def _():
        pl.semaphore_signal(z_in.at[0], inc=1, device_id={"cand": across}, device_id_type=MESH)

    won = win_ref[pair]
    i_won = won == bit
    rival_won = win_ref[rival_pair]
    len_me = len_ref[me]
    len_mate = len_ref[mate]
    len_s = len_ref[2 * pair + won]
    len_c = len_ref[2 * rival_pair + rival_won]
    scale = HD ** (-0.5) * LOG2E
    tail = lax.broadcasted_iota(jnp.int32, (half, HD), 0) + half
    for i, n in enumerate((len_me, len_mate, len_s, len_c)):
        bias[i] = jnp.where(tail < n, 0.0, NEG).astype(jnp.float32)
        for g in range(groups):
            vt[i, g, HD:, :] = jnp.ones((PAD, span), jnp.bfloat16)

    def scores(k, q):
        return lax.dot_general(k, q, (((1,), (1,)), ((), ())), preferred_element_type=jnp.float32)

    def masked(s, i):
        b = bias[i]
        return s[:half], s[half:] + jnp.concatenate([b] * (s.shape[1] // HD), axis=1)

    def key_max(parts):
        peak = parts[0]
        for s in parts[1:]:
            peak = jnp.maximum(peak, s)
        return jnp.max(peak, axis=0, keepdims=True)

    def weighted(parts, peak, v):
        p = jnp.concatenate([jnp.exp2((s - peak) * scale).astype(jnp.bfloat16) for s in parts], axis=0)
        return jnp.dot(v, p, preferred_element_type=jnp.float32)

    def finish(o, first_row, n):
        rows = lax.broadcasted_iota(jnp.int32, (1, o.shape[1]), 1) + first_row
        inverse = jnp.where(rows < n, 1.0 / o[HD : HD + 1], 0.0)
        return jnp.transpose(o[:HD] * inverse).astype(jnp.bfloat16)

    def judged(out, h):
        x = jnp.sum(out.astype(jnp.float32).reshape(-1, 8, HD), axis=0)
        return x * w_ref[h * HD : (h + 1) * HD].reshape(1, HD)

    def pipeline(items, first, rest):
        ahead = first(*items[0])
        for i, item in enumerate(items):
            now = ahead
            if i + 1 < len(items):
                ahead = first(*items[i + 1])
            rest(now, *item)

    def group_blocks(g):
        return [(h, c) for h in range(g * ratio, (g + 1) * ratio) for c in range(0, span, half)]

    for c in loads[: 2 * groups]:
        c.wait()
    for g in range(groups):
        vt[0, g, :HD, :] = jnp.transpose(v_o[g])

    def own_scores(h, c):
        if c == 0:
            loads[2 * groups + h].wait()
        return scores(k_o[h // ratio], q_v[h, c : c + half])

    def own_rest(s, h, c):
        parts = masked(s, 0)
        peak = key_max(parts)
        acc[h, :, c : c + half] = weighted(parts, peak, vt[0, h // ratio])
        top[h, :, c : c + half] = jnp.broadcast_to(peak, (8, half))

    pipeline([b for g in range(groups) for b in group_blocks(g)], own_scores, own_rest)

    @pl.when(hd == 1)
    def _():
        pl.semaphore_wait(z_in.at[0], 1)
        pl.semaphore_signal(core_in.at[0], inc=1, device_id={"head": 0}, device_id_type=MESH)

    @pl.when(hd == 0)
    def _():
        pl.semaphore_wait(core_in.at[0], 1)

    sums = {i: jnp.zeros((8, HD), jnp.float32) for i in (1, 2, 3)}

    def mate_scores(h, c):
        return scores(k_x[h // ratio], q_v[h, c : c + half])

    def mate_rest(s, h, c):
        parts = masked(s, 1)
        before = top[h, :1, c : c + half]
        peak = jnp.maximum(before, key_max(parts))
        keep = jnp.exp2((before - peak) * scale)
        o = weighted(parts, peak, vt[1, h // ratio]) + acc[h, :, c : c + half] * keep
        out = finish(o, c, len_me)
        o_1[h, c : c + half] = out
        sums[1] += judged(out, h)

    for g in range(groups):
        for j in range(2):
            x_copies[2 * g + j].wait_recv()
        k_s[g] = jnp.where(i_won, k_o[g], k_x[g])
        v_s[g] = jnp.where(i_won, v_o[g], v_x[g])
        vt[1, g, :HD, :] = jnp.transpose(v_x[g])
        for j in range(2):
            f_copies[2 * g + j].start()
        pipeline(group_blocks(g), mate_scores, mate_rest)
    part_1[...] = sums[1]


    def second_scores(i):
        h, r, n = chunks[i]
        g = h // ratio
        q_copies[i].wait_recv()
        rows = pl.ds(pl.multiple_of(bit * half + r, quarter), n)
        q = jnp.where(i_won, q_v[h, rows, :], q_x[h, r : r + n])
        return scores(k_s[g], q), scores(k_c[g], q)

    def second_rest(s, i):
        h, r, n = chunks[i]
        g = h // ratio
        a, b = masked(s[0], 2), masked(s[1], 3)
        peak = key_max(a + b)
        o = weighted(a, peak, vt[2, g]) + weighted(b, peak, vt[3, g])
        out = finish(o, bit * half + r, len_s)
        o_2[h, r : r + n] = out
        if h < early:
            sums[2] += judged(out, h)

    def ahead_scores(h, c):
        return scores(k_c[h // ratio], q_v[h, c : c + half])

    def ahead_rest(s, h, c):
        parts = masked(s, 3)
        before = top[h, :1, c : c + half]
        peak = jnp.maximum(before, key_max(parts))
        keep = jnp.exp2((before - peak) * scale)
        o = weighted(parts, peak, vt[3, h // ratio]) + acc[h, :, c : c + half] * keep
        sums[3] += judged(finish(o, c, len_me), h)

    def over(x, n):
        return x / jnp.full((8, HD), n.astype(jnp.float32))

    early = heads - min(3, ratio)
    send_1 = remote(part_1, got_1, ps.at[0], pr.at[0], {"head": other})
    send_2 = remote(part_2, got_2, ps.at[1], pr.at[1], {"head": other})
    send_3 = remote(part_3, got_3, ps.at[2], pr.at[2], {"cand": mate})
    for g in range(groups):
        vt[2, g, :HD, :] = jnp.where(i_won, vt[0, g, :HD, :], vt[1, g, :HD, :])
        for j in range(2):
            f_copies[2 * g + j].wait_recv()
        vt[3, g, :HD, :] = jnp.transpose(v_c[g])
        if g == 0:
            send_1.start()
        pipeline(
            [(i,) for i, (h, _, _) in enumerate(chunks) if h // ratio == g and h < early],
            second_scores, second_rest,
        )
    pipeline(
        [(h, c) for h in range(early, heads) for c in range(0, span, half)],
        ahead_scores, ahead_rest,
    )
    part_2[...] = sums[2] + jnp.where(i_won, sums[3], 0.0)
    late = [(i,) for i, (h, _, _) in enumerate(chunks) if h >= early]
    pipeline(late[:1], second_scores, second_rest)
    send_2.start()
    send_1.wait()
    judged_ref[0] = over(part_1[...] + got_1[...], len_me)
    pipeline(late[1:2], second_scores, second_rest)
    send_2.wait()
    part_3[...] = part_2[...] + got_2[...]
    send_3.start()
    pipeline(late[2:], second_scores, second_rest)
    for c in x_copies + f_copies + q_copies:
        c.wait_send()
    send_3.wait()
    judged_ref[1] = over(part_3[...] + got_3[...], len_s)


def put_out(heads, o_1, o_2, judged_ref, first_hbm, second_hbm, s1_hbm, s2_hbm, s1, s2, sem):
    copies = []
    for h in range(heads):
        cols = pl.ds(h * HD, HD)
        copies.append(pltpu.make_async_copy(o_1.at[h], first_hbm.at[:, cols], sem.at[h]))
        copies.append(pltpu.make_async_copy(o_2.at[h], second_hbm.at[:, cols], sem.at[heads + h]))
    for c in copies:
        c.start()
    for i, (s, dst) in enumerate(((s1, s1_hbm), (s2, s2_hbm))):
        s[0] = jnp.sum(judged_ref[i])
        copies.append(pltpu.make_async_copy(s, dst, sem.at[2 * heads + i]))
        copies[-1].start()
    for c in copies:
        c.wait()


def body(queries, keys, values, lengths, winners, score_weight):
    span = queries.shape[0]
    half = span // 2
    heads = queries.shape[1] // HD
    groups = keys.shape[1] // HD
    bf16, f32 = jnp.bfloat16, jnp.float32
    hbm = pl.BlockSpec(memory_space=pl.ANY)
    vmem = pl.BlockSpec(memory_space=pltpu.VMEM)
    dma = pltpu.SemaphoreType.DMA
    kv = pltpu.VMEM((groups, span, HD), bf16)
    o_1, o_2, judged = pl.pallas_call(
        functools.partial(kernel, heads, groups, span),
        out_shape=(
            OUT((heads, span, HD), bf16),
            OUT((heads, half, HD), bf16),
            OUT((2, 8, HD), f32),
        ),
        in_specs=[hbm] * 6,
        out_specs=(vmem,) * 3,
        scratch_shapes=[
            pltpu.VMEM((heads, span, HD), bf16),
            kv, kv, kv, kv,
            pltpu.VMEM((heads, half, HD), bf16),
            kv, kv, kv, kv,
            pltpu.VMEM((4, groups, HD + PAD, span), bf16),
            pltpu.VMEM((4, half, HD), f32),
            pltpu.VMEM((heads, HD + PAD, span), f32),
            pltpu.VMEM((heads, 8, span), f32),
            pltpu.SMEM(lengths.shape, jnp.int32),
            pltpu.SMEM(winners.shape, jnp.int32),
            pltpu.VMEM(score_weight.shape, f32),
            *[pltpu.VMEM((8, HD), f32)] * 6,
            dma((2 * groups + heads,)),
            dma((2 * groups,)), dma((2 * groups,)),
            dma((2 * groups,)), dma((2 * groups,)),
            dma((heads + 1,)), dma((heads + 1,)),
            dma((3,)),
            dma((3,)), dma((3,)),
            pltpu.SemaphoreType.REGULAR((1,)), pltpu.SemaphoreType.REGULAR((1,)),
        ],
        compiler_params=pltpu.CompilerParams(collective_id=0, has_side_effects=True),
    )(queries, keys, values, lengths, winners, score_weight)
    return pl.pallas_call(
        functools.partial(put_out, heads),
        out_shape=(
            jax.ShapeDtypeStruct(queries.shape, bf16),
            jax.ShapeDtypeStruct((half, queries.shape[1]), bf16),
            jax.ShapeDtypeStruct((1,), f32),
            jax.ShapeDtypeStruct((1,), f32),
        ),
        in_specs=[vmem] * 3,
        out_specs=(hbm,) * 4,
        scratch_shapes=[pltpu.SMEM((1,), f32)] * 2 + [dma((2 * heads + 2,))],
        compiler_params=pltpu.CompilerParams(vmem_limit_bytes=1 << 20),
    )(*(pltpu.with_memory_space_constraint(x, pltpu.VMEM) for x in (o_1, o_2, judged)))


def solution(mesh):
    in_specs = (
        P(("grp", "cand"), "head"),
        P(("grp", "cand"), "head"),
        P(("grp", "cand"), "head"),
        P("grp"),
        P("grp"),
        P("head"),
    )
    out_specs = (
        P(("grp", "cand"), "head"),
        P(("grp", "cand"), "head"),
        P(("grp", "cand")),
        P(("grp", "cand")),
    )
    return jax.shard_map(body, mesh=mesh, in_specs=in_specs, out_specs=out_specs, check_vma=False)
```

```python
import functools

import jax
import jax.numpy as jnp
from jax import lax
from jax.experimental import pallas as pl
from jax.experimental.pallas import tpu as pltpu
from jax.sharding import PartitionSpec as P

HD = 128
LOG2E = 1.4426950408889634
MESH = pl.DeviceIdType.MESH
NEG = -1e30
PAD = 16
OUT = pltpu.VMEM


def kernel(
    heads, groups, span,
    q_hbm, k_hbm, v_hbm, len_hbm, win_hbm, w_hbm,
    o_1, o_2, judged_ref,
    q_v, k_o, v_o, k_x, v_x, q_x, k_s, k_c, v_s, v_c, vt, bias,
    acc, top, len_ref, win_ref, w_ref, part_1, part_2, part_3, got_1, got_2, got_3,
    load_sem, xs, xr, zs, zr, qs, qr, small_sem, ps, pr, z_in, core_in,
):
    half = span // 2
    ratio = heads // groups
    me = lax.axis_index("cand")
    bit = lax.rem(me, 2)
    hd = lax.axis_index("head")
    pair = me // 2
    mate = me + 1 - 2 * bit
    pair_bit = lax.rem(pair, 2)
    rival_pair = pair + 1 - 2 * pair_bit
    across = 2 * rival_pair + bit
    other = 1 - hd

    barrier = pltpu.get_barrier_semaphore()
    pl.semaphore_signal(barrier, inc=1, device_id={"cand": mate}, device_id_type=MESH)
    pl.semaphore_signal(
        barrier, inc=1, device_id={"cand": jnp.where(hd == 0, me, across), "head": 1},
        device_id_type=MESH,
    )

    def col(i):
        return pl.ds(pl.multiple_of(i * HD, HD), HD)

    loads = []
    for g in range(groups):
        loads.append(pltpu.make_async_copy(k_hbm.at[:, col(g)], k_o.at[g], load_sem.at[2 * g]))
        loads.append(pltpu.make_async_copy(v_hbm.at[:, col(g)], v_o.at[g], load_sem.at[2 * g + 1]))
    for h in range(heads):
        loads.append(
            pltpu.make_async_copy(q_hbm.at[:, col(h)], q_v.at[h], load_sem.at[2 * groups + h])
        )
    small = [
        pltpu.make_async_copy(src, dst, small_sem.at[i])
        for i, (src, dst) in enumerate(((len_hbm, len_ref), (win_hbm, win_ref), (w_hbm, w_ref)))
    ]
    pl.semaphore_wait(barrier, 1 + 2 * hd)

    def remote(src, dst, s, r, peer):
        return pltpu.make_async_remote_copy(
            src_ref=src, dst_ref=dst, send_sem=s, recv_sem=r,
            device_id=peer, device_id_type=MESH,
        )

    x_copies, f_copies = [], []
    for g in range(groups):
        for j, (src, dst, fsrc, fdst) in enumerate(
            ((k_hbm, k_x, k_s, k_c), (v_hbm, v_x, v_s, v_c))
        ):
            i = 2 * g + j
            x_copies.append(
                remote(src.at[:, col(g)], dst.at[g], xs.at[i], xr.at[i], {"cand": mate})
            )
            f_copies.append(remote(fsrc.at[g], fdst.at[g], zs.at[i], zr.at[i], {"cand": across}))

    quarter = half // 2
    chunks = [(h, 0, half) for h in range(heads - 1)]
    chunks += [(heads - 1, r, quarter) for r in (0, quarter)]
    q_copies = []
    for i, (h, r, n) in enumerate(chunks):
        rows = pl.ds(pl.multiple_of((1 - bit) * half + r, quarter), n)
        q_copies.append(
            remote(q_hbm.at[rows, col(h)], q_x.at[h, r : r + n], qs.at[i], qr.at[i], {"cand": mate})
        )

    for c in x_copies:
        c.start()
    for c in small + loads:
        c.start()
    for c in q_copies:
        c.start()

    @pl.when(hd == 1)
    def _():
        pl.semaphore_signal(z_in.at[0], inc=1, device_id={"cand": across}, device_id_type=MESH)
        pl.semaphore_wait(z_in.at[0], 1)
        pl.semaphore_signal(core_in.at[0], inc=1, device_id={"head": 0}, device_id_type=MESH)

    for c in small:
        c.wait()

    won = win_ref[pair]
    i_won = won == bit
    rival_won = win_ref[rival_pair]
    len_me = len_ref[me]
    len_mate = len_ref[mate]
    len_s = len_ref[2 * pair + won]
    len_c = len_ref[2 * rival_pair + rival_won]
    scale = HD ** (-0.5) * LOG2E
    tail = lax.broadcasted_iota(jnp.int32, (half, HD), 0) + half
    for i, n in enumerate((len_me, len_mate, len_s, len_c)):
        bias[i] = jnp.where(tail < n, 0.0, NEG).astype(jnp.float32)
        for g in range(groups):
            vt[i, g, HD:, :] = jnp.ones((PAD, span), jnp.bfloat16)

    def scores(k, q):
        return lax.dot_general(k, q, (((1,), (1,)), ((), ())), preferred_element_type=jnp.float32)

    def masked(s, i):
        b = bias[i]
        return s[:half], s[half:] + jnp.concatenate([b] * (s.shape[1] // HD), axis=1)

    def key_max(parts):
        peak = parts[0]
        for s in parts[1:]:
            peak = jnp.maximum(peak, s)
        return jnp.max(peak, axis=0, keepdims=True)

    def weighted(parts, peak, v):
        p = jnp.concatenate([jnp.exp2((s - peak) * scale).astype(jnp.bfloat16) for s in parts], axis=0)
        return jnp.dot(v, p, preferred_element_type=jnp.float32)

    def finish(o, first_row, n):
        rows = lax.broadcasted_iota(jnp.int32, (1, o.shape[1]), 1) + first_row
        inverse = jnp.where(rows < n, 1.0 / o[HD : HD + 1], 0.0)
        return jnp.transpose(o[:HD] * inverse).astype(jnp.bfloat16)

    def judged(out, h):
        x = jnp.sum(out.astype(jnp.float32).reshape(-1, 8, HD), axis=0)
        return x * w_ref[h * HD : (h + 1) * HD].reshape(1, HD)

    def pipeline(items, first, rest):
        ahead = first(*items[0])
        for i, item in enumerate(items):
            now = ahead
            if i + 1 < len(items):
                ahead = first(*items[i + 1])
            rest(now, *item)

    def group_blocks(g):
        return [(h, c) for h in range(g * ratio, (g + 1) * ratio) for c in range(0, span, half)]

    for c in loads[: 2 * groups]:
        c.wait()
    for g in range(groups):
        vt[0, g, :HD, :] = jnp.transpose(v_o[g])

    def own_scores(h, c):
        if c == 0:
            loads[2 * groups + h].wait()
        return scores(k_o[h // ratio], q_v[h, c : c + half])

    def own_rest(s, h, c):
        parts = masked(s, 0)
        peak = key_max(parts)
        acc[h, :, c : c + half] = weighted(parts, peak, vt[0, h // ratio])
        top[h, :, c : c + half] = jnp.broadcast_to(peak, (8, half))

    def forward_k(g):
        x_copies[2 * g].wait_recv()
        k_s[g] = jnp.where(i_won, k_o[g], k_x[g])
        f_copies[2 * g].start()

    def forward_v(g):
        x_copies[2 * g + 1].wait_recv()
        v_s[g] = jnp.where(i_won, v_o[g], v_x[g])
        f_copies[2 * g + 1].start()
        vt[1, g, :HD, :] = jnp.transpose(v_x[g])

    pipeline(group_blocks(0), own_scores, own_rest)

    @pl.when(hd == 0)
    def _():
        pl.semaphore_wait(core_in.at[0], 1)

    forward_k(0)
    pipeline([b for g in range(1, groups) for b in group_blocks(g)], own_scores, own_rest)

    sums = {i: jnp.zeros((8, HD), jnp.float32) for i in (1, 2, 3)}

    def mate_scores(h, c):
        return scores(k_x[h // ratio], q_v[h, c : c + half])

    def mate_rest(s, h, c):
        parts = masked(s, 1)
        before = top[h, :1, c : c + half]
        peak = jnp.maximum(before, key_max(parts))
        keep = jnp.exp2((before - peak) * scale)
        o = weighted(parts, peak, vt[1, h // ratio]) + acc[h, :, c : c + half] * keep
        out = finish(o, c, len_me)
        o_1[h, c : c + half] = out
        sums[1] += judged(out, h)

    for g in range(groups):
        if g:
            forward_k(g)
        forward_v(g)
        pipeline(group_blocks(g), mate_scores, mate_rest)
    part_1[...] = sums[1]

    def second_scores(i):
        h, r, n = chunks[i]
        g = h // ratio
        q_copies[i].wait_recv()
        rows = pl.ds(pl.multiple_of(bit * half + r, quarter), n)
        q = jnp.where(i_won, q_v[h, rows, :], q_x[h, r : r + n])
        return scores(k_s[g], q), scores(k_c[g], q)

    def second_rest(s, i):
        h, r, n = chunks[i]
        g = h // ratio
        a, b = masked(s[0], 2), masked(s[1], 3)
        peak = key_max(a + b)
        o = weighted(a, peak, vt[2, g]) + weighted(b, peak, vt[3, g])
        out = finish(o, bit * half + r, len_s)
        o_2[h, r : r + n] = out
        if h < early:
            sums[2] += judged(out, h)

    def ahead_scores(h, c):
        return scores(k_c[h // ratio], q_v[h, c : c + half])

    def ahead_rest(s, h, c):
        parts = masked(s, 3)
        before = top[h, :1, c : c + half]
        peak = jnp.maximum(before, key_max(parts))
        keep = jnp.exp2((before - peak) * scale)
        o = weighted(parts, peak, vt[3, h // ratio]) + acc[h, :, c : c + half] * keep
        sums[3] += judged(finish(o, c, len_me), h)

    def over(x, n):
        return x / jnp.full((8, HD), n.astype(jnp.float32))

    early = heads - ratio
    send_1 = remote(part_1, got_1, ps.at[0], pr.at[0], {"head": other})
    send_2 = remote(part_2, got_2, ps.at[1], pr.at[1], {"head": other})
    send_3 = remote(part_3, got_3, ps.at[2], pr.at[2], {"cand": mate})

    def challenger(g):
        vt[2, g, :HD, :] = jnp.where(i_won, vt[0, g, :HD, :], vt[1, g, :HD, :])
        for j in range(2):
            f_copies[2 * g + j].wait_recv()
        vt[3, g, :HD, :] = jnp.transpose(v_c[g])

    def second(first, end):
        for i in range(first, end):
            second_rest(second_scores(i), i)

    ahead = early // 2 + 1
    challenger(0)
    send_1.start()
    second(0, ahead)
    for g in range(1, groups):
        challenger(g)
    pipeline(
        [(h, c) for h in range(early, heads) for c in range(0, span, half)],
        ahead_scores, ahead_rest,
    )
    second(ahead, early)
    part_2[...] = sums[2] + jnp.where(i_won, sums[3], 0.0)
    send_1.wait()
    judged_ref[0] = over(part_1[...] + got_1[...], len_me)
    send_2.start()
    second(early, early + 2)
    send_2.wait()
    part_3[...] = part_2[...] + got_2[...]
    second(early + 2, early + 3)
    send_3.start()
    second(early + 3, len(chunks))
    for c in x_copies + f_copies + q_copies:
        c.wait_send()
    send_3.wait()
    judged_ref[1] = over(part_3[...] + got_3[...], len_s)


def put_out(heads, o_1, o_2, judged_ref, first_hbm, second_hbm, s1_hbm, s2_hbm, s1, s2, sem):
    copies = []
    for h in range(heads):
        cols = pl.ds(h * HD, HD)
        copies.append(pltpu.make_async_copy(o_1.at[h], first_hbm.at[:, cols], sem.at[h]))
        copies.append(pltpu.make_async_copy(o_2.at[h], second_hbm.at[:, cols], sem.at[heads + h]))
    for c in copies:
        c.start()
    for i, (s, dst) in enumerate(((s1, s1_hbm), (s2, s2_hbm))):
        s[0] = jnp.sum(judged_ref[i])
        copies.append(pltpu.make_async_copy(s, dst, sem.at[2 * heads + i]))
        copies[-1].start()
    for c in copies:
        c.wait()


def body(queries, keys, values, lengths, winners, score_weight):
    span = queries.shape[0]
    half = span // 2
    heads = queries.shape[1] // HD
    groups = keys.shape[1] // HD
    bf16, f32 = jnp.bfloat16, jnp.float32
    hbm = pl.BlockSpec(memory_space=pl.ANY)
    vmem = pl.BlockSpec(memory_space=pltpu.VMEM)
    dma = pltpu.SemaphoreType.DMA
    kv = pltpu.VMEM((groups, span, HD), bf16)
    o_1, o_2, judged = pl.pallas_call(
        functools.partial(kernel, heads, groups, span),
        out_shape=(
            OUT((heads, span, HD), bf16),
            OUT((heads, half, HD), bf16),
            OUT((2, 8, HD), f32),
        ),
        in_specs=[hbm] * 6,
        out_specs=(vmem,) * 3,
        scratch_shapes=[
            pltpu.VMEM((heads, span, HD), bf16),
            kv, kv, kv, kv,
            pltpu.VMEM((heads, half, HD), bf16),
            kv, kv, kv, kv,
            pltpu.VMEM((4, groups, HD + PAD, span), bf16),
            pltpu.VMEM((4, half, HD), f32),
            pltpu.VMEM((heads, HD + PAD, span), f32),
            pltpu.VMEM((heads, 8, span), f32),
            pltpu.SMEM(lengths.shape, jnp.int32),
            pltpu.SMEM(winners.shape, jnp.int32),
            pltpu.VMEM(score_weight.shape, f32),
            *[pltpu.VMEM((8, HD), f32)] * 6,
            dma((2 * groups + heads,)),
            dma((2 * groups,)), dma((2 * groups,)),
            dma((2 * groups,)), dma((2 * groups,)),
            dma((heads + 1,)), dma((heads + 1,)),
            dma((3,)),
            dma((3,)), dma((3,)),
            pltpu.SemaphoreType.REGULAR((1,)), pltpu.SemaphoreType.REGULAR((1,)),
        ],
        compiler_params=pltpu.CompilerParams(collective_id=0, has_side_effects=True),
    )(queries, keys, values, lengths, winners, score_weight)
    return pl.pallas_call(
        functools.partial(put_out, heads),
        out_shape=(
            jax.ShapeDtypeStruct(queries.shape, bf16),
            jax.ShapeDtypeStruct((half, queries.shape[1]), bf16),
            jax.ShapeDtypeStruct((1,), f32),
            jax.ShapeDtypeStruct((1,), f32),
        ),
        in_specs=[vmem] * 3,
        out_specs=(hbm,) * 4,
        scratch_shapes=[pltpu.SMEM((1,), f32)] * 2 + [dma((2 * heads + 2,))],
        compiler_params=pltpu.CompilerParams(vmem_limit_bytes=1 << 20),
    )(*(pltpu.with_memory_space_constraint(x, pltpu.VMEM) for x in (o_1, o_2, judged)))


def solution(mesh):
    in_specs = (
        P(("grp", "cand"), "head"),
        P(("grp", "cand"), "head"),
        P(("grp", "cand"), "head"),
        P("grp"),
        P("grp"),
        P("head"),
    )
    out_specs = (
        P(("grp", "cand"), "head"),
        P(("grp", "cand"), "head"),
        P(("grp", "cand")),
        P(("grp", "cand")),
    )
    return jax.shard_map(body, mesh=mesh, in_specs=in_specs, out_specs=out_specs, check_vma=False)
```

```python
import functools

import jax
import jax.numpy as jnp
from jax import lax
from jax.experimental import pallas as pl
from jax.experimental.pallas import tpu as pltpu
from jax.sharding import PartitionSpec as P

HD = 128
LOG2E = 1.4426950408889634
MESH = pl.DeviceIdType.MESH
NEG = -1e30
OUT = pltpu.VMEM


def kernel(
    heads, groups, span,
    q_hbm, k_hbm, v_hbm, len_hbm, win_hbm, w_hbm,
    o_1, o_2, judged_ref,
    q_v, k_o, v_o, k_x, v_x, q_x, k_s, k_c, v_s, v_c, vt, bias,
    acc, top, len_ref, win_ref, w_ref, part_1, part_2, got_1, got_2, got_3,
    load_sem, xs, xr, zs, zr, qs, qr, small_sem, ps, pr, z_in, core_in,
):
    half = span // 2
    ratio = heads // groups
    pad = vt.shape[2] - HD
    me = lax.axis_index("cand")
    bit = lax.rem(me, 2)
    hd = lax.axis_index("head")
    pair = me // 2
    mate = me + 1 - 2 * bit
    pair_bit = lax.rem(pair, 2)
    rival_pair = pair + 1 - 2 * pair_bit
    across = 2 * rival_pair + bit
    other = 1 - hd

    barrier = pltpu.get_barrier_semaphore()
    pl.semaphore_signal(barrier, inc=1, device_id={"cand": mate}, device_id_type=MESH)
    pl.semaphore_signal(
        barrier, inc=1, device_id={"cand": jnp.where(hd == 0, me, across), "head": 1},
        device_id_type=MESH,
    )

    def col(i):
        return pl.ds(pl.multiple_of(i * HD, HD), HD)

    loads = []
    for g in range(groups):
        loads.append(pltpu.make_async_copy(k_hbm.at[:, col(g)], k_o.at[g], load_sem.at[2 * g]))
        loads.append(pltpu.make_async_copy(v_hbm.at[:, col(g)], v_o.at[g], load_sem.at[2 * g + 1]))
    for h in range(heads):
        loads.append(
            pltpu.make_async_copy(q_hbm.at[:, col(h)], q_v.at[h], load_sem.at[2 * groups + h])
        )
    small = [
        pltpu.make_async_copy(src, dst, small_sem.at[i])
        for i, (src, dst) in enumerate(((len_hbm, len_ref), (win_hbm, win_ref), (w_hbm, w_ref)))
    ]
    pl.semaphore_wait(barrier, 1 + 2 * hd)

    def remote(src, dst, s, r, peer):
        return pltpu.make_async_remote_copy(
            src_ref=src, dst_ref=dst, send_sem=s, recv_sem=r,
            device_id=peer, device_id_type=MESH,
        )

    x_copies, f_copies = [], []
    for g in range(groups):
        for j, (src, dst, fsrc, fdst) in enumerate(
            ((k_hbm, k_x, k_s, k_c), (v_hbm, v_x, v_s, v_c))
        ):
            i = 2 * g + j
            x_copies.append(
                remote(src.at[:, col(g)], dst.at[g], xs.at[i], xr.at[i], {"cand": mate})
            )
            f_copies.append(remote(fsrc.at[g], fdst.at[g], zs.at[i], zr.at[i], {"cand": across}))

    quarter = half // 2
    chunks = [(h, 0, half) for h in range(heads - 1)]
    chunks += [(heads - 1, r, quarter) for r in (0, quarter)]
    q_copies = []
    for i, (h, r, n) in enumerate(chunks):
        rows = pl.ds(pl.multiple_of((1 - bit) * half + r, quarter), n)
        q_copies.append(
            remote(q_hbm.at[rows, col(h)], q_x.at[h, r : r + n], qs.at[i], qr.at[i], {"cand": mate})
        )

    for c in x_copies:
        c.start()
    for c in small + loads:
        c.start()
    for c in q_copies:
        c.start()

    @pl.when(hd == 1)
    def _():
        pl.semaphore_signal(z_in.at[0], inc=1, device_id={"cand": across}, device_id_type=MESH)
        pl.semaphore_wait(z_in.at[0], 1)
        pl.semaphore_signal(core_in.at[0], inc=1, device_id={"head": 0}, device_id_type=MESH)

    for c in small:
        c.wait()

    won = win_ref[pair]
    i_won = won == bit
    rival_won = win_ref[rival_pair]
    len_me = len_ref[me]
    len_mate = len_ref[mate]
    len_s = len_ref[2 * pair + won]
    len_c = len_ref[2 * rival_pair + rival_won]
    scale = HD ** (-0.5) * LOG2E
    tail = lax.broadcasted_iota(jnp.int32, (half, HD), 0) + half
    for i, n in enumerate((len_me, len_mate, len_s, len_c)):
        bias[i] = jnp.where(tail < n, 0.0, NEG).astype(jnp.float32)

    spare = lax.broadcasted_iota(jnp.int32, (pad, HD), 0)
    scorer = []
    for g in range(groups):
        w = jnp.zeros((pad, HD), jnp.float32)
        for j in range(ratio):
            h = g * ratio + j
            here = (spare == 1 + j) | (spare == 1 + ratio + j)
            w = jnp.where(here, w_ref[h * HD : (h + 1) * HD].reshape(1, HD), w)
        high = w.astype(jnp.bfloat16)
        scorer.append((high, (w - high.astype(jnp.float32)).astype(jnp.bfloat16)))

    def fill_vt(i, g, v):
        t = jnp.transpose(v)
        vt[i, g, :HD, :] = t
        u = sum(jnp.dot(w, t, preferred_element_type=jnp.float32) for w in scorer[g])
        high = u.astype(jnp.bfloat16).astype(jnp.float32)
        row = lax.broadcasted_iota(jnp.int32, u.shape, 0)
        u = jnp.where(row == 0, 1.0, jnp.where(row <= ratio, high, u - high))
        vt[i, g, HD:, :] = u.astype(jnp.bfloat16)

    def scores(k, q):
        return lax.dot_general(k, q, (((1,), (1,)), ((), ())), preferred_element_type=jnp.float32)

    def masked(s, i):
        b = bias[i]
        return s[:half], s[half:] + jnp.concatenate([b] * (s.shape[1] // HD), axis=1)

    def key_max(parts):
        peak = parts[0]
        for s in parts[1:]:
            peak = jnp.maximum(peak, s)
        return jnp.max(peak, axis=0, keepdims=True)

    def weighted(parts, peak, v):
        p = jnp.concatenate([jnp.exp2((s - peak) * scale).astype(jnp.bfloat16) for s in parts], axis=0)
        return jnp.dot(v, p, preferred_element_type=jnp.float32)

    def inverse(total, first_row, n):
        rows = lax.broadcasted_iota(jnp.int32, total.shape, 1) + first_row
        return jnp.where(rows < n, 1.0 / total, 0.0)

    def finish(o, scaled):
        return jnp.transpose(o[:HD] * scaled).astype(jnp.bfloat16)

    def judged(o, scaled, h):
        row = lax.broadcasted_iota(jnp.int32, o.shape, 0)
        j = h % ratio
        x = jnp.where((row == 1 + j) | (row == 1 + ratio + j), o, 0.0) * scaled
        x = sum(x[:, i : i + HD] for i in range(0, x.shape[1], HD))
        return sum(x[i : i + 8] for i in range(0, pad, 8))

    def pipeline(items, first, rest):
        ahead = first(*items[0])
        for i, item in enumerate(items):
            now = ahead
            if i + 1 < len(items):
                ahead = first(*items[i + 1])
            rest(now, *item)

    def group_blocks(g):
        return [(h, c) for h in range(g * ratio, (g + 1) * ratio) for c in range(0, span, half)]

    for c in loads[: 2 * groups]:
        c.wait()
    for g in range(groups):
        fill_vt(0, g, v_o[g])

    def own_scores(h, c):
        if c == 0:
            loads[2 * groups + h].wait()
        return scores(k_o[h // ratio], q_v[h, c : c + half])

    def own_rest(s, h, c):
        parts = masked(s, 0)
        peak = key_max(parts)
        acc[h, :, c : c + half] = weighted(parts, peak, vt[0, h // ratio])
        top[h, :, c : c + half] = jnp.broadcast_to(peak, (8, half))

    def forward_k(g):
        x_copies[2 * g].wait_recv()
        k_s[g] = jnp.where(i_won, k_o[g], k_x[g])
        f_copies[2 * g].start()

    def forward_v(g):
        x_copies[2 * g + 1].wait_recv()
        v_s[g] = jnp.where(i_won, v_o[g], v_x[g])
        f_copies[2 * g + 1].start()
        fill_vt(1, g, v_x[g])

    pipeline(group_blocks(0), own_scores, own_rest)

    @pl.when(hd == 0)
    def _():
        pl.semaphore_wait(core_in.at[0], 1)

    forward_k(0)
    pipeline([b for g in range(1, groups) for b in group_blocks(g)], own_scores, own_rest)

    sums = {i: jnp.zeros((8, HD), jnp.float32) for i in (1, 2, 3)}

    def mate_scores(h, c):
        return scores(k_x[h // ratio], q_v[h, c : c + half])

    def mate_rest(s, h, c):
        parts = masked(s, 1)
        before = top[h, :1, c : c + half]
        peak = jnp.maximum(before, key_max(parts))
        keep = jnp.exp2((before - peak) * scale)
        o = weighted(parts, peak, vt[1, h // ratio]) + acc[h, :, c : c + half] * keep
        scaled = inverse(o[HD : HD + 1], c, len_me)
        o_1[h, c : c + half] = finish(o, scaled)
        sums[1] += judged(o[HD:], scaled, h)

    for g in range(groups):
        if g:
            forward_k(g)
        forward_v(g)
        pipeline(group_blocks(g), mate_scores, mate_rest)
    part_1[...] = sums[1]

    def second_scores(i):
        h, r, n = chunks[i]
        g = h // ratio
        q_copies[i].wait_recv()
        rows = pl.ds(pl.multiple_of(bit * half + r, quarter), n)
        q = jnp.where(i_won, q_v[h, rows, :], q_x[h, r : r + n])
        return scores(k_s[g], q), scores(k_c[g], q)

    def second_rest(s, i):
        h, r, n = chunks[i]
        g = h // ratio
        a, b = masked(s[0], 2), masked(s[1], 3)
        peak = key_max(a + b)
        o = weighted(a, peak, vt[2, g]) + weighted(b, peak, vt[3, g])
        scaled = inverse(o[HD : HD + 1], bit * half + r, len_s)
        o_2[h, r : r + n] = finish(o, scaled)
        if h < early:
            sums[2] += judged(o[HD:], scaled, h)

    def ahead_scores(h, c):
        return scores(k_c[h // ratio], q_v[h, c : c + half])

    def ahead_rest(s, h, c):
        parts = masked(s, 3)
        before = top[h, :1, c : c + half]
        peak = jnp.maximum(before, key_max(parts))
        keep = jnp.exp2((before - peak) * scale)
        o = weighted(parts, peak, vt[3, h // ratio, HD:, :]) + acc[h, HD:, c : c + half] * keep
        sums[3] += judged(o, inverse(o[:1], c, len_me), h)

    def over(x, n):
        return x / jnp.full((8, HD), n.astype(jnp.float32))

    send_1 = remote(part_1, got_1, ps.at[0], pr.at[0], {"head": other})
    send_2 = remote(part_2, got_2, ps.at[1], pr.at[1], {"head": other})
    send_3 = [
        remote(x, got_3.at[i], ps.at[2 + i], pr.at[2 + i], {"cand": mate})
        for i, x in enumerate((part_2, got_2))
    ]

    def second(first, end):
        for i in range(first, end):
            second_rest(second_scores(i), i)

    early = heads - ratio - 1
    send_1.start()
    for g in range(groups):
        vt[2, g] = jnp.where(i_won, vt[0, g], vt[1, g])
        for j in range(2):
            f_copies[2 * g + j].wait_recv()
        fill_vt(3, g, v_c[g])
        pipeline([b for b in group_blocks(g) if b[0] >= early], ahead_scores, ahead_rest)
        if g == 0:
            second(0, early)
    part_2[...] = sums[2] + jnp.where(i_won, sums[3], 0.0)
    send_1.wait()
    judged_ref[0] = over(part_1[...] + got_1[...], len_me)
    send_2.start()
    send_3[0].start()
    second(early, early + 3)
    send_2.wait_recv()
    send_3[1].start()
    second(early + 3, len(chunks))
    for c in x_copies + f_copies + q_copies + [send_2]:
        c.wait_send()
    for c in send_3:
        c.wait()
    judged_ref[1] = over((part_2[...] + got_2[...]) + (got_3[0] + got_3[1]), len_s)


def put_out(heads, o_1, o_2, judged_ref, first_hbm, second_hbm, s1_hbm, s2_hbm, s1, s2, sem):
    copies = []
    for h in range(heads):
        cols = pl.ds(h * HD, HD)
        copies.append(pltpu.make_async_copy(o_1.at[h], first_hbm.at[:, cols], sem.at[h]))
        copies.append(pltpu.make_async_copy(o_2.at[h], second_hbm.at[:, cols], sem.at[heads + h]))
    for c in copies:
        c.start()
    for i, (s, dst) in enumerate(((s1, s1_hbm), (s2, s2_hbm))):
        s[0] = jnp.sum(judged_ref[i])
        copies.append(pltpu.make_async_copy(s, dst, sem.at[2 * heads + i]))
        copies[-1].start()
    for c in copies:
        c.wait()


def body(queries, keys, values, lengths, winners, score_weight):
    span = queries.shape[0]
    half = span // 2
    heads = queries.shape[1] // HD
    groups = keys.shape[1] // HD
    bf16, f32 = jnp.bfloat16, jnp.float32
    hbm = pl.BlockSpec(memory_space=pl.ANY)
    vmem = pl.BlockSpec(memory_space=pltpu.VMEM)
    dma = pltpu.SemaphoreType.DMA
    kv = pltpu.VMEM((groups, span, HD), bf16)
    pad = pl.cdiv(1 + 2 * (heads // groups), 16) * 16
    o_1, o_2, judged = pl.pallas_call(
        functools.partial(kernel, heads, groups, span),
        out_shape=(
            OUT((heads, span, HD), bf16),
            OUT((heads, half, HD), bf16),
            OUT((2, 8, HD), f32),
        ),
        in_specs=[hbm] * 6,
        out_specs=(vmem,) * 3,
        scratch_shapes=[
            pltpu.VMEM((heads, span, HD), bf16),
            kv, kv, kv, kv,
            pltpu.VMEM((heads, half, HD), bf16),
            kv, kv, kv, kv,
            pltpu.VMEM((4, groups, HD + pad, span), bf16),
            pltpu.VMEM((4, half, HD), f32),
            pltpu.VMEM((heads, HD + pad, span), f32),
            pltpu.VMEM((heads, 8, span), f32),
            pltpu.SMEM(lengths.shape, jnp.int32),
            pltpu.SMEM(winners.shape, jnp.int32),
            pltpu.VMEM(score_weight.shape, f32),
            *[pltpu.VMEM((8, HD), f32)] * 4,
            pltpu.VMEM((2, 8, HD), f32),
            dma((2 * groups + heads,)),
            dma((2 * groups,)), dma((2 * groups,)),
            dma((2 * groups,)), dma((2 * groups,)),
            dma((heads + 1,)), dma((heads + 1,)),
            dma((3,)),
            dma((4,)), dma((4,)),
            pltpu.SemaphoreType.REGULAR((1,)), pltpu.SemaphoreType.REGULAR((1,)),
        ],
        compiler_params=pltpu.CompilerParams(collective_id=0, has_side_effects=True),
    )(queries, keys, values, lengths, winners, score_weight)
    return pl.pallas_call(
        functools.partial(put_out, heads),
        out_shape=(
            jax.ShapeDtypeStruct(queries.shape, bf16),
            jax.ShapeDtypeStruct((half, queries.shape[1]), bf16),
            jax.ShapeDtypeStruct((1,), f32),
            jax.ShapeDtypeStruct((1,), f32),
        ),
        in_specs=[vmem] * 3,
        out_specs=(hbm,) * 4,
        scratch_shapes=[pltpu.SMEM((1,), f32)] * 2 + [dma((2 * heads + 2,))],
        compiler_params=pltpu.CompilerParams(vmem_limit_bytes=1 << 20),
    )(*(pltpu.with_memory_space_constraint(x, pltpu.VMEM) for x in (o_1, o_2, judged)))


def solution(mesh):
    in_specs = (
        P(("grp", "cand"), "head"),
        P(("grp", "cand"), "head"),
        P(("grp", "cand"), "head"),
        P("grp"),
        P("grp"),
        P("head"),
    )
    out_specs = (
        P(("grp", "cand"), "head"),
        P(("grp", "cand"), "head"),
        P(("grp", "cand")),
        P(("grp", "cand")),
    )
    return jax.shard_map(body, mesh=mesh, in_specs=in_specs, out_specs=out_specs, check_vma=False)
```

```python
import functools

import jax
import jax.numpy as jnp
from jax import lax
from jax.experimental import pallas as pl
from jax.experimental.pallas import tpu as pltpu
from jax.sharding import PartitionSpec as P

HD = 128
LOG2E = 1.4426950408889634
MESH = pl.DeviceIdType.MESH
NEG = -1e30
OUT = pltpu.VMEM


def kernel(
    heads, groups, span,
    q_hbm, k_hbm, v_hbm, len_hbm, win_hbm, w_hbm,
    o_1, o_2, judged_ref,
    q_v, k_o, v_o, k_x, v_x, q_x, k_s, k_c, v_s, v_c, vt, bias,
    acc, top, len_ref, win_ref, w_ref, part_1, part_2, got_1, got_2,
    load_sem, xs, xr, zs, zr, qs, qr, small_sem, ps, pr, z_in, core_in,
):
    half = span // 2
    ratio = heads // groups
    pad = vt.shape[2] - HD
    me = lax.axis_index("cand")
    bit = lax.rem(me, 2)
    hd = lax.axis_index("head")
    pair = me // 2
    mate = me + 1 - 2 * bit
    pair_bit = lax.rem(pair, 2)
    rival_pair = pair + 1 - 2 * pair_bit
    across = 2 * rival_pair + bit
    other = 1 - hd

    barrier = pltpu.get_barrier_semaphore()
    pl.semaphore_signal(barrier, inc=1, device_id={"cand": mate}, device_id_type=MESH)
    pl.semaphore_signal(
        barrier, inc=1, device_id={"cand": jnp.where(hd == 0, me, across), "head": 1},
        device_id_type=MESH,
    )

    def col(i):
        return pl.ds(pl.multiple_of(i * HD, HD), HD)

    loads = []
    for g in range(groups):
        loads.append(pltpu.make_async_copy(k_hbm.at[:, col(g)], k_o.at[g], load_sem.at[2 * g]))
        loads.append(pltpu.make_async_copy(v_hbm.at[:, col(g)], v_o.at[g], load_sem.at[2 * g + 1]))
    for h in range(heads):
        loads.append(
            pltpu.make_async_copy(q_hbm.at[:, col(h)], q_v.at[h], load_sem.at[2 * groups + h])
        )
    small = [
        pltpu.make_async_copy(src, dst, small_sem.at[i])
        for i, (src, dst) in enumerate(((len_hbm, len_ref), (win_hbm, win_ref), (w_hbm, w_ref)))
    ]
    pl.semaphore_wait(barrier, 1 + 2 * hd)

    def remote(src, dst, s, r, peer):
        return pltpu.make_async_remote_copy(
            src_ref=src, dst_ref=dst, send_sem=s, recv_sem=r,
            device_id=peer, device_id_type=MESH,
        )

    x_copies, f_copies = [], []
    for g in range(groups):
        for j, (src, dst, fsrc, fdst) in enumerate(
            ((k_hbm, k_x, k_s, k_c), (v_hbm, v_x, v_s, v_c))
        ):
            i = 2 * g + j
            x_copies.append(
                remote(src.at[:, col(g)], dst.at[g], xs.at[i], xr.at[i], {"cand": mate})
            )
            f_copies.append(remote(fsrc.at[g], fdst.at[g], zs.at[i], zr.at[i], {"cand": across}))

    chunks = [(h, 0, half) for h in range(heads)]
    q_copies = []
    for i, (h, r, n) in enumerate(chunks):
        rows = pl.ds(pl.multiple_of((1 - bit) * half + r, half), n)
        q_copies.append(
            remote(q_hbm.at[rows, col(h)], q_x.at[h, r : r + n], qs.at[i], qr.at[i], {"cand": mate})
        )

    for c in x_copies:
        c.start()
    for c in small + loads:
        c.start()
    for c in q_copies:
        c.start()

    @pl.when(hd == 1)
    def _():
        for i, peer in enumerate((across, mate)):
            pl.semaphore_signal(z_in.at[i], inc=1, device_id={"cand": peer}, device_id_type=MESH)
        for i in range(2):
            pl.semaphore_wait(z_in.at[i], 1)
        pl.semaphore_signal(core_in.at[0], inc=1, device_id={"head": 0}, device_id_type=MESH)

    for c in small:
        c.wait()

    won = win_ref[pair]
    i_won = won == bit
    rival_won = win_ref[rival_pair]
    len_me = len_ref[me]
    len_mate = len_ref[mate]
    len_s = len_ref[2 * pair + won]
    len_c = len_ref[2 * rival_pair + rival_won]
    scale = HD ** (-0.5) * LOG2E
    tail = lax.broadcasted_iota(jnp.int32, (half, HD), 0) + half
    for i, n in enumerate((len_me, len_mate, len_s, len_c)):
        bias[i] = jnp.where(tail < n, 0.0, NEG).astype(jnp.float32)

    spare = lax.broadcasted_iota(jnp.int32, (pad, HD), 0)
    scorer = []
    for g in range(groups):
        w = jnp.zeros((pad, HD), jnp.float32)
        for j in range(ratio):
            h = g * ratio + j
            here = (spare == 1 + j) | (spare == 1 + ratio + j)
            w = jnp.where(here, w_ref[h * HD : (h + 1) * HD].reshape(1, HD), w)
        high = w.astype(jnp.bfloat16)
        scorer.append((high, (w - high.astype(jnp.float32)).astype(jnp.bfloat16)))

    def fill_vt(i, g, v):
        t = jnp.transpose(v)
        vt[i, g, :HD, :] = t
        u = sum(jnp.dot(w, t, preferred_element_type=jnp.float32) for w in scorer[g])
        high = u.astype(jnp.bfloat16).astype(jnp.float32)
        row = lax.broadcasted_iota(jnp.int32, u.shape, 0)
        u = jnp.where(row == 0, 1.0, jnp.where(row <= ratio, high, u - high))
        vt[i, g, HD:, :] = u.astype(jnp.bfloat16)

    def scores(k, q):
        return lax.dot_general(k, q, (((1,), (1,)), ((), ())), preferred_element_type=jnp.float32)

    def masked(s, i):
        b = bias[i]
        return s[:half], s[half:] + jnp.concatenate([b] * (s.shape[1] // HD), axis=1)

    def key_max(parts):
        peak = parts[0]
        for s in parts[1:]:
            peak = jnp.maximum(peak, s)
        return jnp.max(peak, axis=0, keepdims=True)

    def weighted(parts, peak, v):
        p = jnp.concatenate([jnp.exp2((s - peak) * scale).astype(jnp.bfloat16) for s in parts], axis=0)
        return jnp.dot(v, p, preferred_element_type=jnp.float32)

    def inverse(total, first_row, n):
        rows = lax.broadcasted_iota(jnp.int32, total.shape, 1) + first_row
        return jnp.where(rows < n, 1.0 / total, 0.0)

    def finish(o, scaled):
        return jnp.transpose(o[:HD] * scaled).astype(jnp.bfloat16)

    def judged(o, scaled, h):
        row = lax.broadcasted_iota(jnp.int32, o.shape, 0)
        j = h % ratio
        x = jnp.where((row == 1 + j) | (row == 1 + ratio + j), o, 0.0) * scaled
        x = sum(x[:, i : i + HD] for i in range(0, x.shape[1], HD))
        return sum(x[i : i + 8] for i in range(0, pad, 8))

    def pipeline(items, first, rest):
        ahead = first(*items[0])
        for i, item in enumerate(items):
            now = ahead
            if i + 1 < len(items):
                ahead = first(*items[i + 1])
            rest(now, *item)

    def group_blocks(g):
        return [(h, c) for h in range(g * ratio, (g + 1) * ratio) for c in range(0, span, half)]

    for c in loads[: 2 * groups]:
        c.wait()
    for g in range(groups):
        fill_vt(0, g, v_o[g])

    def own_scores(h, c):
        if c == 0:
            loads[2 * groups + h].wait()
        return scores(k_o[h // ratio], q_v[h, c : c + half])

    def own_rest(s, h, c):
        parts = masked(s, 0)
        peak = key_max(parts)
        acc[h, :, c : c + half] = weighted(parts, peak, vt[0, h // ratio])
        top[h, :, c : c + half] = jnp.broadcast_to(peak, (8, half))

    def forward_k(g):
        x_copies[2 * g].wait_recv()
        k_s[g] = jnp.where(i_won, k_o[g], k_x[g])
        f_copies[2 * g].start()

    def forward_v(g):
        x_copies[2 * g + 1].wait_recv()
        v_s[g] = jnp.where(i_won, v_o[g], v_x[g])
        f_copies[2 * g + 1].start()
        fill_vt(1, g, v_x[g])

    pipeline(group_blocks(0), own_scores, own_rest)

    @pl.when(hd == 0)
    def _():
        pl.semaphore_wait(core_in.at[0], 1)

    forward_k(0)
    pipeline([b for g in range(1, groups) for b in group_blocks(g)], own_scores, own_rest)

    sums = {i: jnp.zeros((8, HD), jnp.float32) for i in (1, 2, 3)}

    def mate_scores(h, c):
        return scores(k_x[h // ratio], q_v[h, c : c + half])

    def mate_rest(s, h, c):
        parts = masked(s, 1)
        before = top[h, :1, c : c + half]
        peak = jnp.maximum(before, key_max(parts))
        keep = jnp.exp2((before - peak) * scale)
        o = weighted(parts, peak, vt[1, h // ratio]) + acc[h, :, c : c + half] * keep
        scaled = inverse(o[HD : HD + 1], c, len_me)
        o_1[h, c : c + half] = finish(o, scaled)
        sums[1] += judged(o[HD:], scaled, h)

    for g in range(groups):
        if g:
            forward_k(g)
        forward_v(g)
        pipeline(group_blocks(g), mate_scores, mate_rest)
    part_1[...] = sums[1]

    def second_scores(i):
        h, r, n = chunks[i]
        g = h // ratio
        q_copies[i].wait_recv()
        rows = pl.ds(pl.multiple_of(bit * half + r, half), n)
        q = jnp.where(i_won, q_v[h, rows, :], q_x[h, r : r + n])
        return scores(k_s[g], q), scores(k_c[g], q)

    def second_rest(s, i):
        h, r, n = chunks[i]
        g = h // ratio
        a, b = masked(s[0], 2), masked(s[1], 3)
        peak = key_max(a + b)
        o = weighted(a, peak, vt[2, g]) + weighted(b, peak, vt[3, g])
        scaled = inverse(o[HD : HD + 1], bit * half + r, len_s)
        o_2[h, r : r + n] = finish(o, scaled)
        if h < early:
            sums[2] += judged(o[HD:], scaled, h)

    def ahead_scores(h, c):
        return scores(k_c[h // ratio], q_v[h, c : c + half])

    def ahead_rest(s, h, c):
        parts = masked(s, 3)
        before = top[h, :1, c : c + half]
        peak = jnp.maximum(before, key_max(parts))
        keep = jnp.exp2((before - peak) * scale)
        o = weighted(parts, peak, vt[3, h // ratio, HD:, :]) + acc[h, HD:, c : c + half] * keep
        sums[3] += judged(o, inverse(o[:1], c, len_me), h)

    def over(x, n):
        return x / jnp.full((8, HD), n.astype(jnp.float32))

    send_1 = remote(part_1, got_1, ps.at[0], pr.at[0], {"head": other})
    send_2 = [
        remote(part_2, got_2.at[i], ps.at[1 + i], pr.at[1 + i], peer)
        for i, peer in enumerate(({"head": other}, {"cand": mate}, {"cand": mate, "head": other}))
    ]

    def second(first, end):
        for i in range(first, end):
            second_rest(second_scores(i), i)

    early = heads - ratio - 1
    send_1.start()
    for g in range(groups):
        vt[2, g] = jnp.where(i_won, vt[0, g], vt[1, g])
        for j in range(2):
            f_copies[2 * g + j].wait_recv()
        fill_vt(3, g, v_c[g])
        pipeline([b for b in group_blocks(g) if b[0] >= early], ahead_scores, ahead_rest)
        if g == 0:
            second(0, early)
    part_2[...] = sums[2] + jnp.where(i_won, sums[3], 0.0)
    send_1.wait()
    judged_ref[0] = over(part_1[...] + got_1[...], len_me)
    for c in send_2:
        c.start()
    second(early, len(chunks))
    for c in x_copies + f_copies + q_copies:
        c.wait_send()
    for c in send_2:
        c.wait()
    judged_ref[1] = over((part_2[...] + got_2[0]) + (got_2[1] + got_2[2]), len_s)


def put_out(heads, o_1, o_2, judged_ref, first_hbm, second_hbm, s1_hbm, s2_hbm, s1, s2, sem):
    copies = []
    for h in range(heads):
        cols = pl.ds(h * HD, HD)
        copies.append(pltpu.make_async_copy(o_1.at[h], first_hbm.at[:, cols], sem.at[h]))
        copies.append(pltpu.make_async_copy(o_2.at[h], second_hbm.at[:, cols], sem.at[heads + h]))
    for c in copies:
        c.start()
    for i, (s, dst) in enumerate(((s1, s1_hbm), (s2, s2_hbm))):
        s[0] = jnp.sum(judged_ref[i])
        copies.append(pltpu.make_async_copy(s, dst, sem.at[2 * heads + i]))
        copies[-1].start()
    for c in copies:
        c.wait()


def body(queries, keys, values, lengths, winners, score_weight):
    span = queries.shape[0]
    half = span // 2
    heads = queries.shape[1] // HD
    groups = keys.shape[1] // HD
    bf16, f32 = jnp.bfloat16, jnp.float32
    hbm = pl.BlockSpec(memory_space=pl.ANY)
    vmem = pl.BlockSpec(memory_space=pltpu.VMEM)
    dma = pltpu.SemaphoreType.DMA
    kv = pltpu.VMEM((groups, span, HD), bf16)
    pad = pl.cdiv(1 + 2 * (heads // groups), 16) * 16
    o_1, o_2, judged = pl.pallas_call(
        functools.partial(kernel, heads, groups, span),
        out_shape=(
            OUT((heads, span, HD), bf16),
            OUT((heads, half, HD), bf16),
            OUT((2, 8, HD), f32),
        ),
        in_specs=[hbm] * 6,
        out_specs=(vmem,) * 3,
        scratch_shapes=[
            pltpu.VMEM((heads, span, HD), bf16),
            kv, kv, kv, kv,
            pltpu.VMEM((heads, half, HD), bf16),
            kv, kv, kv, kv,
            pltpu.VMEM((4, groups, HD + pad, span), bf16),
            pltpu.VMEM((4, half, HD), f32),
            pltpu.VMEM((heads, HD + pad, span), f32),
            pltpu.VMEM((heads, 8, span), f32),
            pltpu.SMEM(lengths.shape, jnp.int32),
            pltpu.SMEM(winners.shape, jnp.int32),
            pltpu.VMEM(score_weight.shape, f32),
            *[pltpu.VMEM((8, HD), f32)] * 3,
            pltpu.VMEM((3, 8, HD), f32),
            dma((2 * groups + heads,)),
            dma((2 * groups,)), dma((2 * groups,)),
            dma((2 * groups,)), dma((2 * groups,)),
            dma((heads,)), dma((heads,)),
            dma((3,)),
            dma((4,)), dma((4,)),
            pltpu.SemaphoreType.REGULAR((2,)), pltpu.SemaphoreType.REGULAR((1,)),
        ],
        compiler_params=pltpu.CompilerParams(collective_id=0, has_side_effects=True),
    )(queries, keys, values, lengths, winners, score_weight)
    return pl.pallas_call(
        functools.partial(put_out, heads),
        out_shape=(
            jax.ShapeDtypeStruct(queries.shape, bf16),
            jax.ShapeDtypeStruct((half, queries.shape[1]), bf16),
            jax.ShapeDtypeStruct((1,), f32),
            jax.ShapeDtypeStruct((1,), f32),
        ),
        in_specs=[vmem] * 3,
        out_specs=(hbm,) * 4,
        scratch_shapes=[pltpu.SMEM((1,), f32)] * 2 + [dma((2 * heads + 2,))],
        compiler_params=pltpu.CompilerParams(vmem_limit_bytes=1 << 20),
    )(*(pltpu.with_memory_space_constraint(x, pltpu.VMEM) for x in (o_1, o_2, judged)))


def solution(mesh):
    in_specs = (
        P(("grp", "cand"), "head"),
        P(("grp", "cand"), "head"),
        P(("grp", "cand"), "head"),
        P("grp"),
        P("grp"),
        P("head"),
    )
    out_specs = (
        P(("grp", "cand"), "head"),
        P(("grp", "cand"), "head"),
        P(("grp", "cand")),
        P(("grp", "cand")),
    )
    return jax.shard_map(body, mesh=mesh, in_specs=in_specs, out_specs=out_specs, check_vma=False)
```

```python
import functools

import jax
import jax.numpy as jnp
from jax import lax
from jax.experimental import pallas as pl
from jax.experimental.pallas import tpu as pltpu
from jax.sharding import PartitionSpec as P

HD = 128
LOG2E = 1.4426950408889634
MESH = pl.DeviceIdType.MESH
NEG = -1e30
OUT = pltpu.VMEM


def kernel(
    heads, groups, span,
    q_hbm, k_hbm, v_hbm, len_hbm, win_hbm, w_hbm,
    o_1, o_2, judged_ref,
    q_v, k_o, v_o, k_x, v_x, q_x, k_s, k_c, v_s, v_c, vt, bias,
    acc, top, o_r, len_ref, win_ref, w_ref, part_1, part_2, got_1, got_2,
    load_sem, xs, xr, zs, zr, qs, qr, small_sem, ps, pr, z_in, core_in,
):
    half = span // 2
    ratio = heads // groups
    pad = vt.shape[2] - HD
    me = lax.axis_index("cand")
    bit = lax.rem(me, 2)
    hd = lax.axis_index("head")
    pair = me // 2
    mate = me + 1 - 2 * bit
    pair_bit = lax.rem(pair, 2)
    rival_pair = pair + 1 - 2 * pair_bit
    across = 2 * rival_pair + bit
    other = 1 - hd

    barrier = pltpu.get_barrier_semaphore()
    pl.semaphore_signal(barrier, inc=1, device_id={"cand": mate}, device_id_type=MESH)
    pl.semaphore_signal(
        barrier, inc=1, device_id={"cand": jnp.where(hd == 0, me, across), "head": 1},
        device_id_type=MESH,
    )

    def col(i):
        return pl.ds(pl.multiple_of(i * HD, HD), HD)

    loads = []
    for g in range(groups):
        loads.append(pltpu.make_async_copy(k_hbm.at[:, col(g)], k_o.at[g], load_sem.at[2 * g]))
        loads.append(pltpu.make_async_copy(v_hbm.at[:, col(g)], v_o.at[g], load_sem.at[2 * g + 1]))
    for h in range(heads):
        loads.append(
            pltpu.make_async_copy(q_hbm.at[:, col(h)], q_v.at[h], load_sem.at[2 * groups + h])
        )
    small = [
        pltpu.make_async_copy(src, dst, small_sem.at[i])
        for i, (src, dst) in enumerate(((len_hbm, len_ref), (win_hbm, win_ref), (w_hbm, w_ref)))
    ]
    pl.semaphore_wait(barrier, 1 + 2 * hd)

    def remote(src, dst, s, r, peer):
        return pltpu.make_async_remote_copy(
            src_ref=src, dst_ref=dst, send_sem=s, recv_sem=r,
            device_id=peer, device_id_type=MESH,
        )

    x_copies, f_copies = [], []
    for g in range(groups):
        for j, (src, dst, fsrc, fdst) in enumerate(
            ((k_hbm, k_x, k_s, k_c), (v_hbm, v_x, v_s, v_c))
        ):
            i = 2 * g + j
            x_copies.append(
                remote(src.at[:, col(g)], dst.at[g], xs.at[i], xr.at[i], {"cand": mate})
            )
            f_copies.append(remote(fsrc.at[g], fdst.at[g], zs.at[i], zr.at[i], {"cand": across}))

    made = list(range(ratio - 2, ratio))
    asked = [h for h in range(heads) if h not in made]
    late = asked[-3:]
    sent = pl.ds(pl.multiple_of((1 - bit) * half, half), half)
    mine = pl.ds(pl.multiple_of(bit * half, half), half)
    q_copies = {
        h: remote(
            o_r.at[made.index(h), sent] if h in made else q_hbm.at[sent, col(h)],
            q_x.at[h], qs.at[h], qr.at[h], {"cand": mate},
        )
        for h in range(heads)
    }

    for c in x_copies:
        c.start()
    for c in small + loads:
        c.start()
    for h in asked:
        q_copies[h].start()

    @pl.when(hd == 1)
    def _():
        for i, peer in enumerate((across, mate)):
            pl.semaphore_signal(z_in.at[i], inc=1, device_id={"cand": peer}, device_id_type=MESH)
        for i in range(2):
            pl.semaphore_wait(z_in.at[i], 1)
        pl.semaphore_signal(core_in.at[0], inc=1, device_id={"head": 0}, device_id_type=MESH)

    for c in small:
        c.wait()

    won = win_ref[pair]
    i_won = won == bit
    rival_won = win_ref[rival_pair]
    len_me = len_ref[me]
    len_mate = len_ref[mate]
    len_s = len_ref[2 * pair + won]
    len_c = len_ref[2 * rival_pair + rival_won]
    scale = HD ** (-0.5) * LOG2E
    tail = lax.broadcasted_iota(jnp.int32, (half, HD), 0) + half
    for i, n in enumerate((len_me, len_mate, len_s, len_c)):
        bias[i] = jnp.where(tail < n, 0.0, NEG).astype(jnp.float32)

    spare = lax.broadcasted_iota(jnp.int32, (pad, HD), 0)
    scorer = []
    for g in range(groups):
        w = jnp.zeros((pad, HD), jnp.float32)
        for j in range(ratio):
            h = g * ratio + j
            here = (spare == 1 + j) | (spare == 1 + ratio + j)
            w = jnp.where(here, w_ref[h * HD : (h + 1) * HD].reshape(1, HD), w)
        high = w.astype(jnp.bfloat16)
        scorer.append((high, (w - high.astype(jnp.float32)).astype(jnp.bfloat16)))

    def fill_vt(i, g, v):
        t = jnp.transpose(v)
        vt[i, g, :HD, :] = t
        u = sum(jnp.dot(w, t, preferred_element_type=jnp.float32) for w in scorer[g])
        high = u.astype(jnp.bfloat16).astype(jnp.float32)
        row = lax.broadcasted_iota(jnp.int32, u.shape, 0)
        u = jnp.where(row == 0, 1.0, jnp.where(row <= ratio, high, u - high))
        vt[i, g, HD:, :] = u.astype(jnp.bfloat16)

    def scores(k, q):
        return lax.dot_general(k, q, (((1,), (1,)), ((), ())), preferred_element_type=jnp.float32)

    def masked(s, i):
        b = bias[i]
        return s[:half], s[half:] + jnp.concatenate([b] * (s.shape[1] // HD), axis=1)

    def key_max(parts):
        peak = parts[0]
        for s in parts[1:]:
            peak = jnp.maximum(peak, s)
        return jnp.max(peak, axis=0, keepdims=True)

    def weighted(parts, peak, v):
        p = jnp.concatenate([jnp.exp2((s - peak) * scale).astype(jnp.bfloat16) for s in parts], axis=0)
        return jnp.dot(v, p, preferred_element_type=jnp.float32)

    def inverse(total, first_row, n):
        rows = lax.broadcasted_iota(jnp.int32, total.shape, 1) + first_row
        return jnp.where(rows < n, 1.0 / total, 0.0)

    def finish(o, scaled):
        return jnp.transpose(o[:HD] * scaled).astype(jnp.bfloat16)

    def judged(o, scaled, h):
        row = lax.broadcasted_iota(jnp.int32, o.shape, 0)
        j = h % ratio
        x = jnp.where((row == 1 + j) | (row == 1 + ratio + j), o, 0.0) * scaled
        x = sum(x[:, i : i + HD] for i in range(0, x.shape[1], HD))
        return sum(x[i : i + 8] for i in range(0, pad, 8))

    def pipeline(items, first, rest):
        ahead = first(*items[0])
        for i, item in enumerate(items):
            now = ahead
            if i + 1 < len(items):
                ahead = first(*items[i + 1])
            rest(now, *item)

    def group_blocks(g):
        return [(h, c) for h in range(g * ratio, (g + 1) * ratio) for c in range(0, span, half)]

    for c in loads[: 2 * groups]:
        c.wait()
    for g in range(groups):
        fill_vt(0, g, v_o[g])

    def own_scores(h, c):
        if c == 0:
            loads[2 * groups + h].wait()
        return scores(k_o[h // ratio], q_v[h, c : c + half])

    def own_rest(s, h, c):
        parts = masked(s, 0)
        peak = key_max(parts)
        acc[h, :, c : c + half] = weighted(parts, peak, vt[0, h // ratio])
        top[h, :, c : c + half] = jnp.broadcast_to(peak, (8, half))

    def forward_k(g):
        x_copies[2 * g].wait_recv()
        k_s[g] = jnp.where(i_won, k_o[g], k_x[g])
        f_copies[2 * g].start()

    def forward_v(g):
        x_copies[2 * g + 1].wait_recv()
        v_s[g] = jnp.where(i_won, v_o[g], v_x[g])
        f_copies[2 * g + 1].start()
        fill_vt(1, g, v_x[g])

    pipeline(group_blocks(0), own_scores, own_rest)

    @pl.when(hd == 0)
    def _():
        pl.semaphore_wait(core_in.at[0], 1)

    forward_k(0)
    pipeline([b for g in range(1, groups) for b in group_blocks(g)], own_scores, own_rest)

    sums = {i: jnp.zeros((8, HD), jnp.float32) for i in (1, 2, 3)}

    def mate_scores(h, c):
        return scores(k_x[h // ratio], q_v[h, c : c + half])

    def mate_rest(s, h, c):
        parts = masked(s, 1)
        before = top[h, :1, c : c + half]
        peak = jnp.maximum(before, key_max(parts))
        keep = jnp.exp2((before - peak) * scale)
        o = weighted(parts, peak, vt[1, h // ratio]) + acc[h, :, c : c + half] * keep
        scaled = inverse(o[HD : HD + 1], c, len_me)
        o_1[h, c : c + half] = finish(o, scaled)
        sums[1] += judged(o[HD:], scaled, h)

    for g in range(groups):
        if g:
            forward_k(g)
        forward_v(g)
        pipeline(group_blocks(g), mate_scores, mate_rest)
    part_1[...] = sums[1]

    def second(h):
        g = h // ratio
        q_copies[h].wait_recv()
        q = jnp.where(i_won, q_v[h, mine, :], q_x[h])
        a, b = masked(scores(k_s[g], q), 2), masked(scores(k_c[g], q), 3)
        peak = key_max(a + b)
        o = weighted(a, peak, vt[2, g]) + weighted(b, peak, vt[3, g])
        scaled = inverse(o[HD : HD + 1], bit * half, len_s)
        o_2[h] = finish(o, scaled)
        if h not in late:
            sums[2] += judged(o[HD:], scaled, h)

    def ahead_scores(h, c):
        return scores(k_c[h // ratio], q_v[h, c : c + half])

    def ahead_rest(s, h, c):
        parts = masked(s, 3)
        before = top[h, :1, c : c + half]
        peak = jnp.maximum(before, key_max(parts))
        keep = jnp.exp2((before - peak) * scale)
        skip = 0 if h in made else HD
        o = weighted(parts, peak, vt[3, h // ratio, skip:, :])
        o += acc[h, skip:, c : c + half] * keep
        scaled = inverse(o[HD - skip : HD - skip + 1], c, len_me)
        if h in made:
            o_r[made.index(h), c : c + half] = finish(o, scaled)
        sums[3] += judged(o[HD - skip :], scaled, h)

    def ahead(some):
        pipeline([(h, c) for h in some for c in range(0, span, half)], ahead_scores, ahead_rest)

    def over(x, n):
        return x / jnp.full((8, HD), n.astype(jnp.float32))

    send_1 = remote(part_1, got_1, ps.at[0], pr.at[0], {"head": other})
    send_2 = [
        remote(part_2, got_2.at[i], ps.at[1 + i], pr.at[1 + i], peer)
        for i, peer in enumerate(({"head": other}, {"cand": mate}, {"cand": mate, "head": other}))
    ]

    def challenger(g):
        vt[2, g] = jnp.where(i_won, vt[0, g], vt[1, g])
        for j in range(2):
            f_copies[2 * g + j].wait_recv()
        fill_vt(3, g, v_c[g])

    send_1.start()
    challenger(0)
    ahead(made)
    second(asked[0])
    for h in made:
        q_copies[h].start()
    for h in asked[1 : ratio - 2]:
        second(h)
    for g in range(1, groups):
        challenger(g)
    for h in asked[ratio - 2 : -3]:
        second(h)
    ahead(late)
    part_2[...] = sums[2] + jnp.where(i_won, sums[3], 0.0)
    send_1.wait()
    judged_ref[0] = over(part_1[...] + got_1[...], len_me)
    for c in send_2:
        c.start()
    for h in late:
        second(h)
    for i, h in enumerate(made):
        q_copies[h].wait_recv()
        o_2[h] = jnp.where(i_won, o_r[i, mine, :], q_x[h])
    for c in x_copies + f_copies + list(q_copies.values()):
        c.wait_send()
    for c in send_2:
        c.wait()
    judged_ref[1] = over((part_2[...] + got_2[0]) + (got_2[1] + got_2[2]), len_s)


def put_out(heads, o_1, o_2, judged_ref, first_hbm, second_hbm, s1_hbm, s2_hbm, s1, s2, sem):
    copies = []
    for h in range(heads):
        cols = pl.ds(h * HD, HD)
        copies.append(pltpu.make_async_copy(o_1.at[h], first_hbm.at[:, cols], sem.at[h]))
        copies.append(pltpu.make_async_copy(o_2.at[h], second_hbm.at[:, cols], sem.at[heads + h]))
    for c in copies:
        c.start()
    for i, (s, dst) in enumerate(((s1, s1_hbm), (s2, s2_hbm))):
        s[0] = jnp.sum(judged_ref[i])
        copies.append(pltpu.make_async_copy(s, dst, sem.at[2 * heads + i]))
        copies[-1].start()
    for c in copies:
        c.wait()


def body(queries, keys, values, lengths, winners, score_weight):
    span = queries.shape[0]
    half = span // 2
    heads = queries.shape[1] // HD
    groups = keys.shape[1] // HD
    bf16, f32 = jnp.bfloat16, jnp.float32
    hbm = pl.BlockSpec(memory_space=pl.ANY)
    vmem = pl.BlockSpec(memory_space=pltpu.VMEM)
    dma = pltpu.SemaphoreType.DMA
    kv = pltpu.VMEM((groups, span, HD), bf16)
    pad = pl.cdiv(1 + 2 * (heads // groups), 16) * 16
    o_1, o_2, judged = pl.pallas_call(
        functools.partial(kernel, heads, groups, span),
        out_shape=(
            OUT((heads, span, HD), bf16),
            OUT((heads, half, HD), bf16),
            OUT((2, 8, HD), f32),
        ),
        in_specs=[hbm] * 6,
        out_specs=(vmem,) * 3,
        scratch_shapes=[
            pltpu.VMEM((heads, span, HD), bf16),
            kv, kv, kv, kv,
            pltpu.VMEM((heads, half, HD), bf16),
            kv, kv, kv, kv,
            pltpu.VMEM((4, groups, HD + pad, span), bf16),
            pltpu.VMEM((4, half, HD), f32),
            pltpu.VMEM((heads, HD + pad, span), f32),
            pltpu.VMEM((heads, 8, span), f32),
            pltpu.VMEM((2, span, HD), bf16),
            pltpu.SMEM(lengths.shape, jnp.int32),
            pltpu.SMEM(winners.shape, jnp.int32),
            pltpu.VMEM(score_weight.shape, f32),
            *[pltpu.VMEM((8, HD), f32)] * 3,
            pltpu.VMEM((3, 8, HD), f32),
            dma((2 * groups + heads,)),
            dma((2 * groups,)), dma((2 * groups,)),
            dma((2 * groups,)), dma((2 * groups,)),
            dma((heads,)), dma((heads,)),
            dma((3,)),
            dma((4,)), dma((4,)),
            pltpu.SemaphoreType.REGULAR((2,)), pltpu.SemaphoreType.REGULAR((1,)),
        ],
        compiler_params=pltpu.CompilerParams(collective_id=0, has_side_effects=True),
    )(queries, keys, values, lengths, winners, score_weight)
    return pl.pallas_call(
        functools.partial(put_out, heads),
        out_shape=(
            jax.ShapeDtypeStruct(queries.shape, bf16),
            jax.ShapeDtypeStruct((half, queries.shape[1]), bf16),
            jax.ShapeDtypeStruct((1,), f32),
            jax.ShapeDtypeStruct((1,), f32),
        ),
        in_specs=[vmem] * 3,
        out_specs=(hbm,) * 4,
        scratch_shapes=[pltpu.SMEM((1,), f32)] * 2 + [dma((2 * heads + 2,))],
        compiler_params=pltpu.CompilerParams(vmem_limit_bytes=1 << 20),
    )(*(pltpu.with_memory_space_constraint(x, pltpu.VMEM) for x in (o_1, o_2, judged)))


def solution(mesh):
    in_specs = (
        P(("grp", "cand"), "head"),
        P(("grp", "cand"), "head"),
        P(("grp", "cand"), "head"),
        P("grp"),
        P("grp"),
        P("head"),
    )
    out_specs = (
        P(("grp", "cand"), "head"),
        P(("grp", "cand"), "head"),
        P(("grp", "cand")),
        P(("grp", "cand")),
    )
    return jax.shard_map(body, mesh=mesh, in_specs=in_specs, out_specs=out_specs, check_vma=False)
```

```python
import functools

import jax
import jax.numpy as jnp
from jax import lax
from jax.experimental import pallas as pl
from jax.experimental.pallas import tpu as pltpu
from jax.sharding import PartitionSpec as P

HD = 128
LOG2E = 1.4426950408889634
MESH = pl.DeviceIdType.MESH
NEG = -1e30
OUT = pltpu.VMEM


def kernel(
    heads, groups, span,
    q_hbm, k_hbm, v_hbm, len_hbm, win_hbm, w_hbm,
    o_1, o_2, judged_ref,
    q_v, k_o, v_o, k_x, v_x, q_x, k_s, k_c, v_s, v_c, vt, bias,
    acc, top, o_r, len_ref, win_ref, w_ref, part_1, part_2, got_1, got_2,
    load_sem, xs, xr, zs, zr, qs, qr, small_sem, ps, pr, z_in, core_in,
):
    half = span // 2
    ratio = heads // groups
    pad = vt.shape[2] - HD
    me = lax.axis_index("cand")
    bit = lax.rem(me, 2)
    hd = lax.axis_index("head")
    pair = me // 2
    mate = me + 1 - 2 * bit
    pair_bit = lax.rem(pair, 2)
    rival_pair = pair + 1 - 2 * pair_bit
    across = 2 * rival_pair + bit
    other = 1 - hd

    barrier = pltpu.get_barrier_semaphore()
    pl.semaphore_signal(barrier, inc=1, device_id={"cand": mate}, device_id_type=MESH)
    pl.semaphore_signal(
        barrier, inc=1, device_id={"cand": jnp.where(hd == 0, me, across), "head": 1},
        device_id_type=MESH,
    )

    def col(i):
        return pl.ds(pl.multiple_of(i * HD, HD), HD)

    loads = []
    for g in range(groups):
        loads.append(pltpu.make_async_copy(k_hbm.at[:, col(g)], k_o.at[g], load_sem.at[2 * g]))
        loads.append(pltpu.make_async_copy(v_hbm.at[:, col(g)], v_o.at[g], load_sem.at[2 * g + 1]))
    for h in range(heads):
        loads.append(
            pltpu.make_async_copy(q_hbm.at[:, col(h)], q_v.at[h], load_sem.at[2 * groups + h])
        )
    small = [
        pltpu.make_async_copy(src, dst, small_sem.at[i])
        for i, (src, dst) in enumerate(((len_hbm, len_ref), (win_hbm, win_ref), (w_hbm, w_ref)))
    ]
    pl.semaphore_wait(barrier, 1 + 2 * hd)

    def remote(src, dst, s, r, peer):
        return pltpu.make_async_remote_copy(
            src_ref=src, dst_ref=dst, send_sem=s, recv_sem=r,
            device_id=peer, device_id_type=MESH,
        )

    x_copies, f_copies = [], []
    for g in range(groups):
        for j, (src, dst, fsrc, fdst) in enumerate(
            ((k_hbm, k_x, k_s, k_c), (v_hbm, v_x, v_s, v_c))
        ):
            i = 2 * g + j
            x_copies.append(
                remote(src.at[:, col(g)], dst.at[g], xs.at[i], xr.at[i], {"cand": mate})
            )
            f_copies.append(remote(fsrc.at[g], fdst.at[g], zs.at[i], zr.at[i], {"cand": across}))

    made = list(range(ratio - 2, ratio))
    asked = [h for h in range(heads) if h not in made]
    late = asked[-3:]
    sent = pl.ds(pl.multiple_of((1 - bit) * half, half), half)
    mine = pl.ds(pl.multiple_of(bit * half, half), half)
    q_copies = {
        h: remote(
            o_r.at[made.index(h), sent] if h in made else q_hbm.at[sent, col(h)],
            q_x.at[h], qs.at[h], qr.at[h], {"cand": mate},
        )
        for h in range(heads)
    }

    for c in x_copies:
        c.start()
    for c in small + loads:
        c.start()
    for h in asked:
        q_copies[h].start()

    @pl.when(hd == 1)
    def _():
        for i, peer in enumerate((across, mate)):
            pl.semaphore_signal(z_in.at[i], inc=1, device_id={"cand": peer}, device_id_type=MESH)
        for i in range(2):
            pl.semaphore_wait(z_in.at[i], 1)
        pl.semaphore_signal(core_in.at[0], inc=1, device_id={"head": 0}, device_id_type=MESH)

    for c in small:
        c.wait()

    won = win_ref[pair]
    i_won = won == bit
    rival_won = win_ref[rival_pair]
    len_me = len_ref[me]
    len_mate = len_ref[mate]
    len_s = len_ref[2 * pair + won]
    len_c = len_ref[2 * rival_pair + rival_won]
    scale = HD ** (-0.5) * LOG2E
    tail = lax.broadcasted_iota(jnp.int32, (half, HD), 0) + half
    for i, n in enumerate((len_me, len_mate, len_s, len_c)):
        bias[i] = jnp.where(tail < n, 0.0, NEG).astype(jnp.float32)

    spare = lax.broadcasted_iota(jnp.int32, (pad, HD), 0)
    scorer = []
    for g in range(groups):
        w = jnp.zeros((pad, HD), jnp.float32)
        for j in range(ratio):
            h = g * ratio + j
            here = (spare == 1 + j) | (spare == 1 + ratio + j)
            w = jnp.where(here, w_ref[h * HD : (h + 1) * HD].reshape(1, HD), w)
        high = w.astype(jnp.bfloat16)
        scorer.append((high, (w - high.astype(jnp.float32)).astype(jnp.bfloat16)))

    def fill_vt(i, g, v):
        t = jnp.transpose(v)
        vt[i, g, :HD, :] = t
        u = sum(jnp.dot(w, t, preferred_element_type=jnp.float32) for w in scorer[g])
        high = u.astype(jnp.bfloat16).astype(jnp.float32)
        row = lax.broadcasted_iota(jnp.int32, u.shape, 0)
        u = jnp.where(row == 0, 1.0, jnp.where(row <= ratio, high, u - high))
        vt[i, g, HD:, :] = u.astype(jnp.bfloat16)

    def scores(k, q):
        return lax.dot_general(k, q, (((1,), (1,)), ((), ())), preferred_element_type=jnp.float32)

    def masked(s, i):
        b = bias[i]
        return s[:half], s[half:] + jnp.concatenate([b] * (s.shape[1] // HD), axis=1)

    def key_max(parts):
        peak = parts[0]
        for s in parts[1:]:
            peak = jnp.maximum(peak, s)
        return jnp.max(peak, axis=0, keepdims=True)

    def weighted(parts, peak, v):
        p = jnp.concatenate([jnp.exp2((s - peak) * scale).astype(jnp.bfloat16) for s in parts], axis=0)
        return jnp.dot(v, p, preferred_element_type=jnp.float32)

    def inverse(total, first_row, n):
        rows = lax.broadcasted_iota(jnp.int32, total.shape, 1) + first_row
        return jnp.where(rows < n, 1.0 / total, 0.0)

    def finish(o, scaled):
        return jnp.transpose(o[:HD] * scaled).astype(jnp.bfloat16)

    def judged(o, scaled, h):
        row = lax.broadcasted_iota(jnp.int32, o.shape, 0)
        j = h % ratio
        x = jnp.where((row == 1 + j) | (row == 1 + ratio + j), o, 0.0) * scaled
        x = sum(x[:, i : i + HD] for i in range(0, x.shape[1], HD))
        return sum(x[i : i + 8] for i in range(0, pad, 8))

    def pipeline(items, first, rest):
        ahead = first(*items[0])
        for i, item in enumerate(items):
            now = ahead
            if i + 1 < len(items):
                ahead = first(*items[i + 1])
            rest(now, *item)

    def group_blocks(g):
        return [(h, c) for h in range(g * ratio, (g + 1) * ratio) for c in range(0, span, half)]

    for c in loads[: 2 * groups]:
        c.wait()
    for g in range(groups):
        fill_vt(0, g, v_o[g])

    def own_scores(h, c):
        if c == 0:
            loads[2 * groups + h].wait()
        return scores(k_o[h // ratio], q_v[h, c : c + half])

    def own_rest(s, h, c):
        parts = masked(s, 0)
        peak = key_max(parts)
        acc[h, :, c : c + half] = weighted(parts, peak, vt[0, h // ratio])
        top[h, :, c : c + half] = jnp.broadcast_to(peak, (8, half))

    def forward_k(g):
        x_copies[2 * g].wait_recv()
        k_s[g] = jnp.where(i_won, k_o[g], k_x[g])
        f_copies[2 * g].start()

    def forward_v(g):
        x_copies[2 * g + 1].wait_recv()
        v_s[g] = jnp.where(i_won, v_o[g], v_x[g])
        f_copies[2 * g + 1].start()
        fill_vt(1, g, v_x[g])

    pipeline(group_blocks(0), own_scores, own_rest)

    @pl.when(hd == 0)
    def _():
        pl.semaphore_wait(core_in.at[0], 1)

    forward_k(0)
    pipeline([b for g in range(1, groups) for b in group_blocks(g)], own_scores, own_rest)

    sums = {i: jnp.zeros((8, HD), jnp.float32) for i in (1, 2, 3)}

    def mate_scores(h, c):
        return scores(k_x[h // ratio], q_v[h, c : c + half])

    def mate_rest(s, h, c):
        parts = masked(s, 1)
        before = top[h, :1, c : c + half]
        peak = jnp.maximum(before, key_max(parts))
        keep = jnp.exp2((before - peak) * scale)
        o = weighted(parts, peak, vt[1, h // ratio]) + acc[h, :, c : c + half] * keep
        scaled = inverse(o[HD : HD + 1], c, len_me)
        o_1[h, c : c + half] = finish(o, scaled)
        sums[1] += judged(o[HD:], scaled, h)

    for g in range(groups):
        if g:
            forward_k(g)
        forward_v(g)
        pipeline(group_blocks(g), mate_scores, mate_rest)
    part_1[...] = sums[1]

    def second(h):
        g = h // ratio
        q_copies[h].wait_recv()
        q = jnp.where(i_won, q_v[h, mine, :], q_x[h])
        a, b = masked(scores(k_s[g], q), 2), masked(scores(k_c[g], q), 3)
        peak = key_max(a + b)
        o = weighted(a, peak, vt[2, g]) + weighted(b, peak, vt[3, g])
        scaled = inverse(o[HD : HD + 1], bit * half, len_s)
        o_2[h] = finish(o, scaled)
        if h not in late:
            sums[2] += judged(o[HD:], scaled, h)

    def ahead_scores(h, c):
        return scores(k_c[h // ratio], q_v[h, c : c + half])

    def ahead_rest(s, h, c):
        parts = masked(s, 3)
        before = top[h, :1, c : c + half]
        peak = jnp.maximum(before, key_max(parts))
        keep = jnp.exp2((before - peak) * scale)
        skip = 0 if h in made else HD
        o = weighted(parts, peak, vt[3, h // ratio, skip:, :])
        o += acc[h, skip:, c : c + half] * keep
        scaled = inverse(o[HD - skip : HD - skip + 1], c, len_me)
        if h in made:
            o_r[made.index(h), c : c + half] = finish(o, scaled)
        sums[3] += judged(o[HD - skip :], scaled, h)

    def ahead(some):
        pipeline([(h, c) for h in some for c in range(0, span, half)], ahead_scores, ahead_rest)

    def over(x, n):
        return x / jnp.full((8, HD), n.astype(jnp.float32))

    send_1 = remote(part_1, got_1, ps.at[0], pr.at[0], {"head": other})
    send_2 = [
        remote(part_2, got_2.at[i], ps.at[1 + i], pr.at[1 + i], peer)
        for i, peer in enumerate(({"head": other}, {"cand": mate}, {"cand": mate, "head": other}))
    ]

    def challenger(g):
        vt[2, g] = jnp.where(i_won, vt[0, g], vt[1, g])
        for j in range(2):
            f_copies[2 * g + j].wait_recv()
        fill_vt(3, g, v_c[g])

    send_1.start()
    challenger(0)
    ahead(made)
    second(asked[0])
    for h in made[:-1]:
        q_copies[h].start()
    for h in asked[1 : ratio - 2]:
        second(h)
    for g in range(1, groups):
        challenger(g)
    second(asked[ratio - 2])
    ahead(late)
    for h in asked[ratio - 1 : -3]:
        second(h)
    part_2[...] = sums[2] + jnp.where(i_won, sums[3], 0.0)
    send_1.wait()
    judged_ref[0] = over(part_1[...] + got_1[...], len_me)
    for c in send_2:
        c.start()
    q_copies[made[-1]].start()
    for h in late:
        second(h)
    for i, h in enumerate(made):
        q_copies[h].wait_recv()
        o_2[h] = jnp.where(i_won, o_r[i, mine, :], q_x[h])
    for c in x_copies + f_copies + list(q_copies.values()):
        c.wait_send()
    for c in send_2:
        c.wait()
    judged_ref[1] = over((part_2[...] + got_2[0]) + (got_2[1] + got_2[2]), len_s)


def put_out(heads, o_1, o_2, judged_ref, first_hbm, second_hbm, s1_hbm, s2_hbm, s1, s2, sem):
    copies = []
    for h in range(heads):
        cols = pl.ds(h * HD, HD)
        copies.append(pltpu.make_async_copy(o_1.at[h], first_hbm.at[:, cols], sem.at[h]))
        copies.append(pltpu.make_async_copy(o_2.at[h], second_hbm.at[:, cols], sem.at[heads + h]))
    for c in copies:
        c.start()
    for i, (s, dst) in enumerate(((s1, s1_hbm), (s2, s2_hbm))):
        s[0] = jnp.sum(judged_ref[i])
        copies.append(pltpu.make_async_copy(s, dst, sem.at[2 * heads + i]))
        copies[-1].start()
    for c in copies:
        c.wait()


def body(queries, keys, values, lengths, winners, score_weight):
    span = queries.shape[0]
    half = span // 2
    heads = queries.shape[1] // HD
    groups = keys.shape[1] // HD
    bf16, f32 = jnp.bfloat16, jnp.float32
    hbm = pl.BlockSpec(memory_space=pl.ANY)
    vmem = pl.BlockSpec(memory_space=pltpu.VMEM)
    dma = pltpu.SemaphoreType.DMA
    kv = pltpu.VMEM((groups, span, HD), bf16)
    pad = pl.cdiv(1 + 2 * (heads // groups), 16) * 16
    o_1, o_2, judged = pl.pallas_call(
        functools.partial(kernel, heads, groups, span),
        out_shape=(
            OUT((heads, span, HD), bf16),
            OUT((heads, half, HD), bf16),
            OUT((2, 8, HD), f32),
        ),
        in_specs=[hbm] * 6,
        out_specs=(vmem,) * 3,
        scratch_shapes=[
            pltpu.VMEM((heads, span, HD), bf16),
            kv, kv, kv, kv,
            pltpu.VMEM((heads, half, HD), bf16),
            kv, kv, kv, kv,
            pltpu.VMEM((4, groups, HD + pad, span), bf16),
            pltpu.VMEM((4, half, HD), f32),
            pltpu.VMEM((heads, HD + pad, span), f32),
            pltpu.VMEM((heads, 8, span), f32),
            pltpu.VMEM((2, span, HD), bf16),
            pltpu.SMEM(lengths.shape, jnp.int32),
            pltpu.SMEM(winners.shape, jnp.int32),
            pltpu.VMEM(score_weight.shape, f32),
            *[pltpu.VMEM((8, HD), f32)] * 3,
            pltpu.VMEM((3, 8, HD), f32),
            dma((2 * groups + heads,)),
            dma((2 * groups,)), dma((2 * groups,)),
            dma((2 * groups,)), dma((2 * groups,)),
            dma((heads,)), dma((heads,)),
            dma((3,)),
            dma((4,)), dma((4,)),
            pltpu.SemaphoreType.REGULAR((2,)), pltpu.SemaphoreType.REGULAR((1,)),
        ],
        compiler_params=pltpu.CompilerParams(collective_id=0, has_side_effects=True),
    )(queries, keys, values, lengths, winners, score_weight)
    return pl.pallas_call(
        functools.partial(put_out, heads),
        out_shape=(
            jax.ShapeDtypeStruct(queries.shape, bf16),
            jax.ShapeDtypeStruct((half, queries.shape[1]), bf16),
            jax.ShapeDtypeStruct((1,), f32),
            jax.ShapeDtypeStruct((1,), f32),
        ),
        in_specs=[vmem] * 3,
        out_specs=(hbm,) * 4,
        scratch_shapes=[pltpu.SMEM((1,), f32)] * 2 + [dma((2 * heads + 2,))],
        compiler_params=pltpu.CompilerParams(vmem_limit_bytes=1 << 20),
    )(*(pltpu.with_memory_space_constraint(x, pltpu.VMEM) for x in (o_1, o_2, judged)))


def solution(mesh):
    in_specs = (
        P(("grp", "cand"), "head"),
        P(("grp", "cand"), "head"),
        P(("grp", "cand"), "head"),
        P("grp"),
        P("grp"),
        P("head"),
    )
    out_specs = (
        P(("grp", "cand"), "head"),
        P(("grp", "cand"), "head"),
        P(("grp", "cand")),
        P(("grp", "cand")),
    )
    return jax.shard_map(body, mesh=mesh, in_specs=in_specs, out_specs=out_specs, check_vma=False)
```
